32 devices in a mesh: exp: 8 (over z, x), head: 4 (over y, core).
Axes of the slice: x: 2, y: 2, z: 4, core: 2. Of those that a mesh axis runs over, the one named last changes fastest.
Arguments:
- queries: bfloat16 [1024, 4096], P('exp', 'head')
- keys: bfloat16 [1024, 1024], P('exp', 'head')
- values: bfloat16 [1024, 1024], P('exp', 'head')
- w_in: bfloat16 [8, 4096, 2, 768], P('exp', 'head'), may hold values from -0.09375 to 0.09375
- w_out: bfloat16 [8, 768, 4096], P('exp', None, 'head'), may hold values from -0.21875 to 0.21875
- routes: int32 [1024, 6], P('exp'), may hold values from 0 to 7, as said below
- route_weights: float32 [1024, 6], P('exp'), may hold values from 0.05 to 0.45
- grad_out: bfloat16 [1024, 4096], P('exp', 'head'), may hold values from -6 to 6
Outputs:
- output: bfloat16 [1024, 4096], P('exp', 'head')
- grad_attended: bfloat16 [1024, 4096], P('exp', 'head')
The draws below stay inside these ranges and needn't reach their ends.
Inputs may be any that keep to these rules, and one draw needn't show every extreme that they name: `routes`: each row names 6 different experts. In each aligned block of 128 rows (the rows of one index of exp) no expert is named more than 112 times.
All inputs are finite; a program needn't handle non-finite values.
Results may differ from the reference program's by a relative error of at most 0.017.
Values may be sent and summed in bfloat16 or wider, within the bound.
A program may use at most 128 MiB of HBM per device.

```python
import jax
import jax.numpy as jnp
from jax import lax

D = 4096
QUERY_HEADS = 32
KEY_VALUE_HEADS = 8
HEAD_WIDTH = 128
FF = 768
TOP = 6
TOK_DEV = 128
CACHE_PER_INDEX = 128
EXPERTS = 8
WINDOW_TOKENS = 1024
CACHE_POSITIONS = 1024
MEAN_LOAD = 96
CAP = 112


def drawn_keys(key):
    return 1.5 * jax.random.truncated_normal(jax.random.fold_in(key, 11), -4.0, 4.0, (CACHE_POSITIONS, KEY_VALUE_HEADS * HEAD_WIDTH), jnp.float32)


def draw_keys(key, part):
    starting_key_rows = drawn_keys(key)
    return starting_key_rows.astype(jnp.bfloat16)


def draw_queries(key, part):
    unrouted = 1.5 * jax.random.truncated_normal(jax.random.fold_in(key, 13), -4.0, 4.0, (WINDOW_TOKENS, QUERY_HEADS * HEAD_WIDTH), jnp.float32)
    return unrouted.astype(jnp.bfloat16)


def draw_values(key, part):
    unrouted = jax.random.truncated_normal(jax.random.fold_in(key, 17), -4.0, 4.0, (CACHE_POSITIONS, KEY_VALUE_HEADS * HEAD_WIDTH), jnp.float32)
    return unrouted.astype(jnp.bfloat16)


def draw_routes(key, part):
    block_total = WINDOW_TOKENS // TOK_DEV
    spread = CAP - MEAN_LOAD
    order = jax.random.permutation(jax.random.fold_in(key, 21), EXPERTS)

    def one_block(block_key):
        offsets = jax.random.randint(jax.random.fold_in(block_key, 1), (EXPERTS // 2,), 0, spread + 1)
        offsets = offsets.at[0].set(spread)
        signed = jnp.stack([offsets, -offsets], axis=1).reshape(EXPERTS)
        counts = jnp.zeros((EXPERTS,), jnp.int32).at[order].set(MEAN_LOAD + signed)
        ends = jnp.cumsum(counts)
        positions = jnp.arange(TOK_DEV * TOP, dtype=jnp.int32)
        listing = jnp.sum((ends[None, :] <= positions[:, None]).astype(jnp.int32), axis=1)
        table = listing.reshape(TOP, TOK_DEV).T
        ranks = jax.random.randint(jax.random.fold_in(block_key, 3), (TOK_DEV, TOP), 0, 1000) * TOP
        ranks = ranks + jnp.arange(TOP, dtype=jnp.int32)[None, :]
        column_order = jnp.argsort(ranks, axis=1, stable=True)
        table = jnp.take_along_axis(table, column_order, axis=1)
        shuffle = jax.random.permutation(jax.random.fold_in(block_key, 2), TOK_DEV)
        return table[shuffle]
    block_keys = jax.random.split(jax.random.fold_in(key, 22), block_total)
    return jax.vmap(one_block)(block_keys).reshape(WINDOW_TOKENS, TOP).astype(jnp.int32)


def block_levels(own_key, dims, cuts, least, top_value):
    loudness, own = 1.0, jax.random.fold_in(own_key, 6)
    for dim, shards_of in cuts:
        draws = jnp.exp(jax.random.uniform(jax.random.fold_in(own, dim), (shards_of,), jnp.float32, least / len(cuts), top_value / len(cuts)))
        loudness = loudness * jnp.repeat(draws, dims[dim] // shards_of).reshape([-1 if axis == dim else 1 for axis in range(len(dims))])
    return loudness


def normal_values(rng, shape, width, bound, cuts=(), kind=jnp.bfloat16):
    result = jax.random.normal(rng, shape, jnp.float32) * width
    if len(cuts) > 0:
        result = block_levels(rng, shape, cuts, -0.22, 0.18) * result
    return jnp.clip(result, min=-bound, max=bound).astype(kind)


def setup_inputs(seed: int = 0) -> dict:
    key_of = jax.random.split(jax.random.key(seed), 9)
    return {
        "queries": draw_queries(jax.random.fold_in(key_of[8], 71), 0),
        "keys": draw_keys(jax.random.fold_in(key_of[8], 71), 0),
        "values": draw_values(jax.random.fold_in(key_of[8], 71), 0),
        "w_in": normal_values(key_of[3], (EXPERTS, D, 2, FF), D ** -0.5, 0.09375, ((0, 8), (1, 4))),
        "w_out": normal_values(key_of[4], (EXPERTS, FF, D), FF ** -0.5, 0.21875, ((0, 8), (2, 4))),
        "routes": draw_routes(jax.random.fold_in(key_of[8], 71), 0),
        "route_weights": jnp.clip(0.05 + 0.39999999 * jax.random.uniform(key_of[6], (WINDOW_TOKENS, TOP), jnp.float32) ** block_levels(key_of[6], (WINDOW_TOKENS, TOP), ((0, 8),), -0.2, 0.2), 0.05, 0.45),
        "grad_out": normal_values(key_of[7], (WINDOW_TOKENS, D), 1.0, 6.0, ((0, 8), (1, 4))),
    }


norm_eps = 1e-05
hidden_logits = -1e+30

def settle(tensor):
    return lax.optimization_barrier(tensor.astype(jnp.bfloat16)).astype(jnp.float32)

def attend(queries, keys, values):
    grouping_width = QUERY_HEADS // KEY_VALUE_HEADS
    count_of_blocks = CACHE_POSITIONS // CACHE_PER_INDEX
    heads_of_queries = queries.astype(jnp.float32).reshape(WINDOW_TOKENS, KEY_VALUE_HEADS, grouping_width, HEAD_WIDTH)
    blocked_keys = keys.astype(jnp.float32).reshape(count_of_blocks, CACHE_PER_INDEX, KEY_VALUE_HEADS, HEAD_WIDTH)
    blocked_values = values.astype(jnp.float32).reshape(count_of_blocks, CACHE_PER_INDEX, KEY_VALUE_HEADS, HEAD_WIDTH)
    query_pos = CACHE_POSITIONS - WINDOW_TOKENS + jnp.arange(WINDOW_TOKENS, dtype=jnp.int32)

    def one_block(running, element):
        top_now, total_now, sums_now = running
        key_block, value_block, block_index = element
        key_pos = block_index * CACHE_PER_INDEX + jnp.arange(CACHE_PER_INDEX, dtype=jnp.int32)
        visible = (key_pos[None, :] <= query_pos[:, None])[:, None, None, :]
        scores = jnp.einsum('tgid,jgd->tgij', heads_of_queries, key_block) * HEAD_WIDTH ** (-0.5)
        scores = jnp.where(visible, scores, hidden_logits)
        block_top = settle(lax.optimization_barrier(jnp.max(scores, axis=-1)))
        weights = jnp.where(visible, jnp.exp(scores - block_top[..., None]), 0.0)
        block_total = settle(lax.optimization_barrier(jnp.sum(weights, axis=-1)))
        block_sum = settle(jnp.einsum('tgij,jgd->tgid', settle(weights), value_block))
        new_top = jnp.maximum(top_now, block_top)
        old_factor = jnp.exp(top_now - new_top)
        new_factor = jnp.exp(block_top - new_top)
        total_next = total_now * old_factor + block_total * new_factor
        sums_next = sums_now * old_factor[..., None] + block_sum * new_factor[..., None]
        return ((new_top, total_next, sums_next), None)
    beginning = (jnp.full((WINDOW_TOKENS, KEY_VALUE_HEADS, grouping_width), hidden_logits, jnp.float32), jnp.zeros((WINDOW_TOKENS, KEY_VALUE_HEADS, grouping_width), jnp.float32), jnp.zeros((WINDOW_TOKENS, KEY_VALUE_HEADS, grouping_width, HEAD_WIDTH), jnp.float32))
    running, ignored = lax.scan(one_block, beginning, (blocked_keys, blocked_values, jnp.arange(count_of_blocks, dtype=jnp.int32)))
    return (running[2] / running[1][..., None]).reshape(WINDOW_TOKENS, QUERY_HEADS * HEAD_WIDTH).astype(jnp.bfloat16)

def expert_pass(element):
    row_block, grad_block, w_first, w_second = element
    row_float = row_block.astype(jnp.float32)
    squares = lax.optimization_barrier(jnp.sum(row_float * row_float, axis=1))
    norm_scale = lax.rsqrt(squares / D + norm_eps)[:, None]
    raw_sums = jnp.dot(row_block, w_first.reshape(D, 2 * FF), preferred_element_type=jnp.float32).reshape(-1, 2, FF)
    gate_value = raw_sums[:, 0] * norm_scale
    up_value = raw_sums[:, 1] * norm_scale
    gate_sigmoid = jax.nn.sigmoid(gate_value)
    gate_silu = gate_value * gate_sigmoid
    hidden_act = (gate_silu * up_value).astype(jnp.bfloat16)
    out_rows = jnp.dot(hidden_act, w_second, preferred_element_type=jnp.float32).astype(jnp.bfloat16)
    back_sums = jnp.dot(grad_block, jnp.transpose(w_second), preferred_element_type=jnp.float32)
    grad_gate = back_sums * up_value * gate_sigmoid * (1.0 + gate_value * (1.0 - gate_sigmoid))
    grad_up = back_sums * gate_silu
    grad_hidden = jnp.stack([grad_gate, grad_up], axis=1).astype(jnp.bfloat16)
    grad_normed = jnp.dot(grad_hidden.reshape(-1, 2 * FF), jnp.transpose(w_first.reshape(D, 2 * FF)), preferred_element_type=jnp.float32)
    inner_sum = lax.optimization_barrier(jnp.sum(grad_hidden.astype(jnp.float32) * jnp.stack([gate_value, up_value], axis=1), axis=(1, 2)))
    grad_rows = norm_scale * grad_normed - row_float * (norm_scale * norm_scale / D) * inner_sum[:, None]
    return (out_rows, grad_rows.astype(jnp.bfloat16))

def reference(queries, keys, values, w_in, w_out, routes, route_weights, grad_out):
    attended = attend(queries, keys, values)
    shard_count = WINDOW_TOKENS // TOK_DEV
    shard_routes = routes.reshape(shard_count, TOK_DEV * TOP)
    expert_hits = (shard_routes[:, :, None] == jnp.arange(EXPERTS, dtype=jnp.int32)[None, None, :]).astype(jnp.int32)
    earlier = jnp.cumsum(expert_hits, axis=1) - expert_hits
    slot_index = lax.optimization_barrier(jnp.sum(earlier * expert_hits, axis=2)).astype(jnp.int32)
    row_of = (jnp.arange(shard_count, dtype=jnp.int32)[:, None] * CAP + slot_index).reshape(-1).astype(jnp.int32)
    expert_of = shard_routes.reshape(-1).astype(jnp.int32)
    token_of = jnp.repeat(jnp.arange(WINDOW_TOKENS, dtype=jnp.int32), TOP)
    slot_rows = shard_count * CAP
    row_table = jnp.zeros((EXPERTS, slot_rows, D), jnp.bfloat16).at[expert_of, row_of].set(attended[token_of])
    grad_table = jnp.zeros((EXPERTS, slot_rows, D), jnp.bfloat16).at[expert_of, row_of].set(grad_out[token_of])
    out_table, grad_rows = lax.map(expert_pass, (row_table, grad_table, w_in, w_out))
    picked_out = out_table[expert_of, row_of].astype(jnp.float32).reshape(WINDOW_TOKENS, TOP, D)
    picked_grad = grad_rows[expert_of, row_of].astype(jnp.float32).reshape(WINDOW_TOKENS, TOP, D)
    output = (attended.astype(jnp.float32) + lax.optimization_barrier(jnp.sum(route_weights[:, :, None] * picked_out, axis=1))).astype(jnp.bfloat16)
    grad_attended = (grad_out.astype(jnp.float32) + lax.optimization_barrier(jnp.sum(route_weights[:, :, None] * picked_grad, axis=1))).astype(jnp.bfloat16)
    return (output, grad_attended)
```

```python
import jax
import jax.numpy as jnp
from jax import lax
from jax.experimental import pallas as pl
from jax.experimental.pallas import tpu as pltpu
from jax.sharding import PartitionSpec as P

D = 4096
HEAD_WIDTH = 128
TOP = 6


norm_eps = 1e-05
hidden_logits = -1e30


def block_partial(query_rows, query_pos, rows_of_keys, value_rows, key_pos):
    row_count = query_rows.shape[0]
    count_of_blocks = rows_of_keys.shape[0]
    kv_heads = rows_of_keys.shape[2] // HEAD_WIDTH
    grouping_width = query_rows.shape[1] // HEAD_WIDTH // kv_heads
    heads_of_queries = query_rows.reshape(row_count, kv_heads, grouping_width, HEAD_WIDTH)
    key_heads = rows_of_keys.reshape(count_of_blocks, -1, kv_heads, HEAD_WIDTH)
    value_heads = value_rows.reshape(count_of_blocks, -1, kv_heads, HEAD_WIDTH)
    visible = (key_pos[:, None, :] <= query_pos[None, :, None])[:, :, None, None, :]
    scores = jnp.einsum(
        "tgid,bjgd->btgij", heads_of_queries, key_heads, preferred_element_type=jnp.float32
    ) * HEAD_WIDTH ** (-0.5)
    scores = jnp.where(visible, scores, hidden_logits)
    best_score = jnp.max(scores, axis=-1).astype(jnp.bfloat16)
    weights = jnp.where(visible, jnp.exp(scores - best_score.astype(jnp.float32)[..., None]), 0.0)
    weight_total = jnp.sum(weights, axis=-1).astype(jnp.bfloat16)
    weighted_sum = jnp.einsum(
        "btgij,bjgd->btgid",
        weights.astype(jnp.bfloat16),
        value_heads,
        preferred_element_type=jnp.float32,
    ).astype(jnp.bfloat16)
    head_count = kv_heads * grouping_width
    return (
        best_score.reshape(count_of_blocks, row_count, head_count),
        weight_total.reshape(count_of_blocks, row_count, head_count),
        weighted_sum.reshape(count_of_blocks, row_count, head_count * HEAD_WIDTH),
    )


def fold_partials(running, best_score, weight_total, weighted_sum):
    top_now, total_now, sums_now = running
    best_value = best_score.astype(jnp.float32)
    new_top = jnp.maximum(top_now, jnp.max(best_value, axis=0))
    old_factor = jnp.exp(top_now - new_top)
    block_factor = jnp.exp(best_value - new_top[None])
    total_next = total_now * old_factor + jnp.sum(
        weight_total.astype(jnp.float32) * block_factor, axis=0
    )
    spread_sums = weighted_sum.reshape(
        weighted_sum.shape[0], sums_now.shape[0], sums_now.shape[1], HEAD_WIDTH
    )
    sums_next = sums_now * old_factor[..., None] + jnp.sum(
        spread_sums.astype(jnp.float32) * block_factor[..., None], axis=0
    )
    return (new_top, total_next, sums_next)


def per_device(queries, keys, values, w_in, w_out, routes, route_weights, grad_out):
    exp_count = lax.axis_size("exp")
    exp_index = lax.axis_index("exp")
    head_devices = lax.axis_size("head")
    token_count = queries.shape[0]
    query_width = queries.shape[1]
    head_count = query_width // HEAD_WIDTH
    cache_rows = keys.shape[0]
    window = token_count * exp_count
    offset = cache_rows * exp_count - window
    beginning = (
        jnp.full((token_count, head_count), hidden_logits, jnp.float32),
        jnp.zeros((token_count, head_count), jnp.float32),
        jnp.zeros((token_count, head_count, HEAD_WIDTH), jnp.float32),
    )
    own_pos = offset + exp_index * token_count + jnp.arange(token_count, dtype=jnp.int32)
    key_piece = lax.all_gather(keys, "exp", axis=0, tiled=True)
    value_piece = lax.all_gather(values, "exp", axis=0, tiled=True)
    piece_blocks = key_piece.shape[0] // cache_rows
    key_split = key_piece.reshape(piece_blocks, cache_rows, -1)
    value_split = value_piece.reshape(piece_blocks, cache_rows, -1)
    pos_split = jnp.arange(key_piece.shape[0], dtype=jnp.int32).reshape(piece_blocks, cache_rows)

    def one_block(state, element):
        key_block, value_block, pos_block = element
        block_parts = block_partial(
            queries, own_pos, key_block[None], value_block[None], pos_block[None]
        )
        return (fold_partials(state, block_parts[0], block_parts[1], block_parts[2]), None)

    state, ignored = lax.scan(one_block, beginning, (key_split, value_split, pos_split))
    attended = (
        (state[2] / state[1][..., None]).reshape(token_count, query_width).astype(jnp.bfloat16)
    )
    row_width = attended.shape[1]
    experts_all = w_in.shape[0] * exp_count
    mean_load = TOP * token_count // experts_all
    capacity = mean_load + mean_load // 6
    places = experts_all * capacity
    flat_routes = routes.reshape(-1)
    expert_hits = (
        flat_routes[:, None] == jnp.arange(experts_all, dtype=jnp.int32)[None, :]
    ).astype(jnp.int32)
    earlier = jnp.cumsum(expert_hits, axis=0) - expert_hits
    slot_index = jnp.sum(earlier * expert_hits, axis=1)
    place_index = flat_routes * capacity + slot_index
    chosen = (place_index[:, None] == jnp.arange(places, dtype=jnp.int32)[None, :]).astype(
        jnp.bfloat16
    )
    picker = jnp.sum(chosen.reshape(token_count, TOP, places), axis=1)
    contract_rows = (((0,), (0,)), ((), ()))
    send_rows = lax.dot_general(picker, attended, contract_rows, preferred_element_type=jnp.float32)
    send_rows = send_rows.astype(jnp.bfloat16).reshape(experts_all, capacity, row_width)
    send_grads = lax.dot_general(
        picker, grad_out, contract_rows, preferred_element_type=jnp.float32
    )
    send_grads = send_grads.astype(jnp.bfloat16).reshape(experts_all, capacity, row_width)
    w_first = w_in[0]
    w_second = w_out[0]
    rows_in = lax.all_to_all(send_rows, "exp", split_axis=0, concat_axis=0, tiled=True)
    grads_in = lax.all_to_all(send_grads, "exp", split_axis=0, concat_axis=0, tiled=True)
    lead_count, item_count, width_in = rows_in.shape
    row_total = lead_count * item_count
    row_block = rows_in.reshape(row_total, width_in)
    grad_block = grads_in.reshape(row_total, width_in)
    row_float = row_block.astype(jnp.float32)
    raw_sums = jnp.einsum("rd,dkf->rkf", row_block, w_first, preferred_element_type=jnp.float32)
    back_sums = lax.dot_general(
        grad_block, w_second, (((1,), (1,)), ((), ())), preferred_element_type=jnp.float32
    )
    squares = jnp.sum(row_float * row_float, axis=1)
    square_tile = jnp.broadcast_to(squares[:, None, None], (row_total, 1, head_devices))
    raw_part = lax.psum_scatter(raw_sums, "head", scatter_dimension=2, tiled=True)
    back_part = lax.psum_scatter(back_sums[:, None, :], "head", scatter_dimension=2, tiled=True)
    square_part = lax.psum_scatter(square_tile, "head", scatter_dimension=2, tiled=True)
    norm_scale = lax.rsqrt(square_part[:, 0] / D + norm_eps)
    gate_value = raw_part[:, 0] * norm_scale
    up_value = raw_part[:, 1] * norm_scale
    back_value = back_part[:, 0]
    gate_sigmoid = jax.nn.sigmoid(gate_value)
    gate_silu = gate_value * gate_sigmoid
    act_part = (gate_silu * up_value).astype(jnp.bfloat16)
    grad_gate = back_value * up_value * gate_sigmoid * (1.0 + gate_value * (1.0 - gate_sigmoid))
    grad_up = back_value * gate_silu
    grad_part = jnp.stack([grad_gate, grad_up], axis=1).astype(jnp.bfloat16)
    inner_part = jnp.sum(
        grad_part.astype(jnp.float32) * jnp.stack([gate_value, up_value], axis=1), axis=(1, 2)
    )
    act_whole = lax.all_gather(act_part[:, None, :], "head", axis=2, tiled=True)
    grad_hidden = lax.all_gather(grad_part, "head", axis=2, tiled=True)
    hidden_act = act_whole[:, 0]
    inner_sum = lax.psum(inner_part, "head")
    out_rows = jnp.dot(hidden_act, w_second, preferred_element_type=jnp.float32).astype(
        jnp.bfloat16
    )
    grad_normed = jnp.einsum(
        "rkf,dkf->rd", grad_hidden, w_first, preferred_element_type=jnp.float32
    )
    grad_rows = (
        norm_scale * grad_normed - row_float * (norm_scale * norm_scale / D) * inner_sum[:, None]
    )
    expert_out = out_rows.reshape(lead_count, item_count, width_in)
    expert_grad = grad_rows.astype(jnp.bfloat16).reshape(lead_count, item_count, width_in)
    came_out, came_grad = (
        lax.all_to_all(expert_out, "exp", split_axis=0, concat_axis=0, tiled=True),
        lax.all_to_all(expert_grad, "exp", split_axis=0, concat_axis=0, tiled=True),
    )
    picked_out = came_out.reshape(places, row_width)[place_index].reshape(
        token_count, TOP, row_width
    )
    picked_grad = came_grad.reshape(places, row_width)[place_index].reshape(
        token_count, TOP, row_width
    )
    output = attended.astype(jnp.float32) + jnp.sum(
        route_weights[:, :, None] * picked_out.astype(jnp.float32), axis=1
    )
    grad_attended = grad_out.astype(jnp.float32) + jnp.sum(
        route_weights[:, :, None] * picked_grad.astype(jnp.float32), axis=1
    )
    return (output.astype(jnp.bfloat16), grad_attended.astype(jnp.bfloat16))


def attention_kernel(head_count, group, start_ref, q_ref, k_ref, v_ref, o_ref):
    rows = q_ref.shape[0]
    cached = k_ref.shape[0]
    first = start_ref[0]
    row_pos = first + lax.broadcasted_iota(jnp.int32, (rows, cached), 0)
    visible = lax.broadcasted_iota(jnp.int32, (rows, cached), 1) <= row_pos
    for head in range(head_count):
        cols = slice(head * HEAD_WIDTH, (head + 1) * HEAD_WIDTH)
        kv_head = head // group
        kv_cols = slice(kv_head * HEAD_WIDTH, (kv_head + 1) * HEAD_WIDTH)
        scores = lax.dot_general(
            q_ref[:, cols],
            k_ref[:, kv_cols],
            (((1,), (1,)), ((), ())),
            preferred_element_type=jnp.float32,
        ) * HEAD_WIDTH ** (-0.5)
        scores = jnp.where(visible, scores, hidden_logits)
        best = jnp.max(scores, axis=1, keepdims=True)
        weights = jnp.exp(scores - best)
        total = jnp.sum(weights, axis=1, keepdims=True)
        sums = jnp.dot(
            weights.astype(jnp.bfloat16), v_ref[:, kv_cols], preferred_element_type=jnp.float32
        )
        o_ref[:, cols] = (sums / total).astype(jnp.bfloat16)


def attend_local(queries, key_all, value_all, start):
    head_count = queries.shape[1] // HEAD_WIDTH
    group = head_count // (key_all.shape[1] // HEAD_WIDTH)

    def body(*refs):
        attention_kernel(head_count, group, *refs)

    return pl.pallas_call(
        body,
        out_shape=jax.ShapeDtypeStruct(queries.shape, jnp.bfloat16),
        in_specs=[pl.BlockSpec(memory_space=pltpu.SMEM)]
        + [pl.BlockSpec(memory_space=pltpu.VMEM)] * 3,
        out_specs=pl.BlockSpec(memory_space=pltpu.VMEM),
        name="attention",
    )(start.reshape(1).astype(jnp.int32), queries, key_all, value_all)


def three_parts(value):
    high = value.astype(jnp.bfloat16)
    rest = value - high.astype(jnp.float32)
    middle = rest.astype(jnp.bfloat16)
    low = (rest - middle.astype(jnp.float32)).astype(jnp.bfloat16)
    return high, middle, low


def gather_exp(block, tag):
    return lax.all_gather(block, "exp", axis=0, tiled=True)


def dense_device(queries, keys, values, w_in, w_out, routes, route_weights, grad_out):
    exp_count = lax.axis_size("exp")
    exp_index = lax.axis_index("exp")
    parts = lax.axis_size("head")
    tokens, width = queries.shape
    experts = w_in.shape[0] * exp_count
    hidden = w_in.shape[3]
    share = hidden // parts
    kv_width = keys.shape[1]
    offset = keys.shape[0] * exp_count - tokens * exp_count
    w_first = w_in[0]
    w_second = w_out[0]
    kv_all = gather_exp(jnp.concatenate([keys, values], axis=1), 0)
    hits = routes[:, :, None] == jnp.arange(experts, dtype=jnp.int32)[None, None, :]
    table = jnp.sum(jnp.where(hits, route_weights[:, :, None], 0.0), axis=1)
    packed = jnp.concatenate(three_parts(table), axis=1)
    packed = jnp.pad(packed, ((0, 0), (0, -packed.shape[1] % 128)))
    grad_pack = gather_exp(jnp.concatenate([grad_out, packed], axis=1), 1)
    grads = grad_pack[:, :width]
    attended = attend_local(
        queries, kv_all[:, :kv_width], kv_all[:, kv_width:], offset + exp_index * tokens
    )
    rows = gather_exp(attended, 2)
    count = rows.shape[0]
    pieces = grad_pack[:, width : width + 3 * experts].astype(jnp.float32)
    table_all = jnp.sum(pieces.reshape(count, 3, experts), axis=1)
    own = (jnp.arange(experts) == exp_index).astype(jnp.float32)
    gain = jnp.sum(table_all * own[None, :], axis=1)[:, None]
    w_split = w_first.reshape(width, 2, parts, share)
    second_split = w_second.reshape(parts, share, width)
    back_sums = jnp.einsum(
        "rd,hfd->hrf", grads, second_split, preferred_element_type=jnp.float32
    ).astype(jnp.bfloat16)
    back_value = lax.psum_scatter(back_sums, "head", scatter_dimension=0, tiled=False)
    row_float = rows.astype(jnp.float32)
    raw_sums = jnp.einsum("rd,dkhf->hrkf", rows, w_split, preferred_element_type=jnp.float32)
    raw_sums = raw_sums.astype(jnp.bfloat16).reshape(parts, count, 2 * share)
    squares = jnp.sum(row_float * row_float, axis=1)
    square_tile = jnp.broadcast_to(
        squares.astype(jnp.bfloat16)[None, :, None], (parts, count, 128)
    )
    raw_part = lax.psum_scatter(
        jnp.concatenate([raw_sums, square_tile], axis=2),
        "head",
        scatter_dimension=0,
        tiled=False,
    ).astype(jnp.float32)
    norm_scale = lax.rsqrt(raw_part[:, 2 * share : 2 * share + 1] / D + norm_eps)
    gate_value = raw_part[:, :share] * norm_scale
    up_value = raw_part[:, share : 2 * share] * norm_scale
    back_value = back_value.astype(jnp.float32)
    sigmoid = jax.nn.sigmoid(gate_value)
    silu = gate_value * sigmoid
    act = (silu * up_value).astype(jnp.bfloat16)
    grad_gate = (back_value * up_value * sigmoid * (1.0 + gate_value * (1.0 - sigmoid))).astype(
        jnp.bfloat16
    )
    grad_up = (back_value * silu).astype(jnp.bfloat16)
    inner = jnp.sum(
        grad_gate.astype(jnp.float32) * gate_value + grad_up.astype(jnp.float32) * up_value,
        axis=1,
        keepdims=True,
    )
    sent = jnp.concatenate([act, grad_gate, grad_up, *three_parts(inner)], axis=1)
    sent = jnp.pad(sent, ((0, 0), (0, -sent.shape[1] % 128)))
    whole = lax.all_gather(sent, "head", axis=0, tiled=False)
    inner_sum = jnp.sum(whole[:, :, 3 * share : 3 * share + 3].astype(jnp.float32), axis=(0, 2))[
        :, None
    ]
    act_all = jnp.transpose(whole[:, :, :share], (1, 0, 2)).reshape(count, hidden)
    gate_all = jnp.transpose(whole[:, :, share : 2 * share], (1, 0, 2)).reshape(count, hidden)
    up_all = jnp.transpose(whole[:, :, 2 * share : 3 * share], (1, 0, 2)).reshape(count, hidden)
    grad_all = jnp.concatenate([gate_all, up_all], axis=1)
    out_rows = jnp.dot(act_all, w_second, preferred_element_type=jnp.float32)
    grad_normed = lax.dot_general(
        grad_all,
        w_first.reshape(width, 2 * hidden),
        (((1,), (1,)), ((), ())),
        preferred_element_type=jnp.float32,
    )
    grad_rows = norm_scale * grad_normed - row_float * (norm_scale * norm_scale / D) * inner_sum
    routed = gain > 0.0
    both = jnp.concatenate(
        [
            jnp.where(routed, gain * out_rows, 0.0).astype(jnp.bfloat16),
            jnp.where(routed, gain * grad_rows, 0.0).astype(jnp.bfloat16),
        ],
        axis=1,
    )
    summed = lax.psum_scatter(both, "exp", scatter_dimension=0, tiled=True).astype(jnp.float32)
    output = attended.astype(jnp.float32) + summed[:, :width]
    grad_attended = grad_out.astype(jnp.float32) + summed[:, width:]
    return (output.astype(jnp.bfloat16), grad_attended.astype(jnp.bfloat16))


def solution(mesh):
    dense = 2 * TOP >= mesh.shape["exp"]
    in_specs = (
        P("exp", "head"),
        P("exp", "head"),
        P("exp", "head"),
        P("exp", "head", None, None),
        P("exp", None, "head"),
        P("exp", None),
        P("exp", None),
        P("exp", "head"),
    )
    out_specs = (P("exp", "head"), P("exp", "head"))
    return jax.shard_map(
        dense_device if dense else per_device, mesh=mesh, in_specs=in_specs, out_specs=out_specs, check_vma=False
    )
```

```python
import jax
import jax.numpy as jnp
from jax import lax
from jax.experimental import pallas as pl
from jax.experimental.pallas import tpu as pltpu
from jax.sharding import PartitionSpec as P

D = 4096
HEAD_WIDTH = 128
TOP = 6


norm_eps = 1e-05
hidden_logits = -1e30


def block_partial(query_rows, query_pos, rows_of_keys, value_rows, key_pos):
    row_count = query_rows.shape[0]
    count_of_blocks = rows_of_keys.shape[0]
    kv_heads = rows_of_keys.shape[2] // HEAD_WIDTH
    grouping_width = query_rows.shape[1] // HEAD_WIDTH // kv_heads
    heads_of_queries = query_rows.reshape(row_count, kv_heads, grouping_width, HEAD_WIDTH)
    key_heads = rows_of_keys.reshape(count_of_blocks, -1, kv_heads, HEAD_WIDTH)
    value_heads = value_rows.reshape(count_of_blocks, -1, kv_heads, HEAD_WIDTH)
    visible = (key_pos[:, None, :] <= query_pos[None, :, None])[:, :, None, None, :]
    scores = jnp.einsum(
        "tgid,bjgd->btgij", heads_of_queries, key_heads, preferred_element_type=jnp.float32
    ) * HEAD_WIDTH ** (-0.5)
    scores = jnp.where(visible, scores, hidden_logits)
    best_score = jnp.max(scores, axis=-1).astype(jnp.bfloat16)
    weights = jnp.where(visible, jnp.exp(scores - best_score.astype(jnp.float32)[..., None]), 0.0)
    weight_total = jnp.sum(weights, axis=-1).astype(jnp.bfloat16)
    weighted_sum = jnp.einsum(
        "btgij,bjgd->btgid",
        weights.astype(jnp.bfloat16),
        value_heads,
        preferred_element_type=jnp.float32,
    ).astype(jnp.bfloat16)
    head_count = kv_heads * grouping_width
    return (
        best_score.reshape(count_of_blocks, row_count, head_count),
        weight_total.reshape(count_of_blocks, row_count, head_count),
        weighted_sum.reshape(count_of_blocks, row_count, head_count * HEAD_WIDTH),
    )


def fold_partials(running, best_score, weight_total, weighted_sum):
    top_now, total_now, sums_now = running
    best_value = best_score.astype(jnp.float32)
    new_top = jnp.maximum(top_now, jnp.max(best_value, axis=0))
    old_factor = jnp.exp(top_now - new_top)
    block_factor = jnp.exp(best_value - new_top[None])
    total_next = total_now * old_factor + jnp.sum(
        weight_total.astype(jnp.float32) * block_factor, axis=0
    )
    spread_sums = weighted_sum.reshape(
        weighted_sum.shape[0], sums_now.shape[0], sums_now.shape[1], HEAD_WIDTH
    )
    sums_next = sums_now * old_factor[..., None] + jnp.sum(
        spread_sums.astype(jnp.float32) * block_factor[..., None], axis=0
    )
    return (new_top, total_next, sums_next)


def per_device(queries, keys, values, w_in, w_out, routes, route_weights, grad_out):
    exp_count = lax.axis_size("exp")
    exp_index = lax.axis_index("exp")
    head_devices = lax.axis_size("head")
    token_count = queries.shape[0]
    query_width = queries.shape[1]
    head_count = query_width // HEAD_WIDTH
    cache_rows = keys.shape[0]
    window = token_count * exp_count
    offset = cache_rows * exp_count - window
    beginning = (
        jnp.full((token_count, head_count), hidden_logits, jnp.float32),
        jnp.zeros((token_count, head_count), jnp.float32),
        jnp.zeros((token_count, head_count, HEAD_WIDTH), jnp.float32),
    )
    own_pos = offset + exp_index * token_count + jnp.arange(token_count, dtype=jnp.int32)
    key_piece = lax.all_gather(keys, "exp", axis=0, tiled=True)
    value_piece = lax.all_gather(values, "exp", axis=0, tiled=True)
    piece_blocks = key_piece.shape[0] // cache_rows
    key_split = key_piece.reshape(piece_blocks, cache_rows, -1)
    value_split = value_piece.reshape(piece_blocks, cache_rows, -1)
    pos_split = jnp.arange(key_piece.shape[0], dtype=jnp.int32).reshape(piece_blocks, cache_rows)

    def one_block(state, element):
        key_block, value_block, pos_block = element
        block_parts = block_partial(
            queries, own_pos, key_block[None], value_block[None], pos_block[None]
        )
        return (fold_partials(state, block_parts[0], block_parts[1], block_parts[2]), None)

    state, ignored = lax.scan(one_block, beginning, (key_split, value_split, pos_split))
    attended = (
        (state[2] / state[1][..., None]).reshape(token_count, query_width).astype(jnp.bfloat16)
    )
    row_width = attended.shape[1]
    experts_all = w_in.shape[0] * exp_count
    mean_load = TOP * token_count // experts_all
    capacity = mean_load + mean_load // 6
    places = experts_all * capacity
    flat_routes = routes.reshape(-1)
    expert_hits = (
        flat_routes[:, None] == jnp.arange(experts_all, dtype=jnp.int32)[None, :]
    ).astype(jnp.int32)
    earlier = jnp.cumsum(expert_hits, axis=0) - expert_hits
    slot_index = jnp.sum(earlier * expert_hits, axis=1)
    place_index = flat_routes * capacity + slot_index
    chosen = (place_index[:, None] == jnp.arange(places, dtype=jnp.int32)[None, :]).astype(
        jnp.bfloat16
    )
    picker = jnp.sum(chosen.reshape(token_count, TOP, places), axis=1)
    contract_rows = (((0,), (0,)), ((), ()))
    send_rows = lax.dot_general(picker, attended, contract_rows, preferred_element_type=jnp.float32)
    send_rows = send_rows.astype(jnp.bfloat16).reshape(experts_all, capacity, row_width)
    send_grads = lax.dot_general(
        picker, grad_out, contract_rows, preferred_element_type=jnp.float32
    )
    send_grads = send_grads.astype(jnp.bfloat16).reshape(experts_all, capacity, row_width)
    w_first = w_in[0]
    w_second = w_out[0]
    rows_in = lax.all_to_all(send_rows, "exp", split_axis=0, concat_axis=0, tiled=True)
    grads_in = lax.all_to_all(send_grads, "exp", split_axis=0, concat_axis=0, tiled=True)
    lead_count, item_count, width_in = rows_in.shape
    row_total = lead_count * item_count
    row_block = rows_in.reshape(row_total, width_in)
    grad_block = grads_in.reshape(row_total, width_in)
    row_float = row_block.astype(jnp.float32)
    raw_sums = jnp.einsum("rd,dkf->rkf", row_block, w_first, preferred_element_type=jnp.float32)
    back_sums = lax.dot_general(
        grad_block, w_second, (((1,), (1,)), ((), ())), preferred_element_type=jnp.float32
    )
    squares = jnp.sum(row_float * row_float, axis=1)
    square_tile = jnp.broadcast_to(squares[:, None, None], (row_total, 1, head_devices))
    raw_part = lax.psum_scatter(raw_sums, "head", scatter_dimension=2, tiled=True)
    back_part = lax.psum_scatter(back_sums[:, None, :], "head", scatter_dimension=2, tiled=True)
    square_part = lax.psum_scatter(square_tile, "head", scatter_dimension=2, tiled=True)
    norm_scale = lax.rsqrt(square_part[:, 0] / D + norm_eps)
    gate_value = raw_part[:, 0] * norm_scale
    up_value = raw_part[:, 1] * norm_scale
    back_value = back_part[:, 0]
    gate_sigmoid = jax.nn.sigmoid(gate_value)
    gate_silu = gate_value * gate_sigmoid
    act_part = (gate_silu * up_value).astype(jnp.bfloat16)
    grad_gate = back_value * up_value * gate_sigmoid * (1.0 + gate_value * (1.0 - gate_sigmoid))
    grad_up = back_value * gate_silu
    grad_part = jnp.stack([grad_gate, grad_up], axis=1).astype(jnp.bfloat16)
    inner_part = jnp.sum(
        grad_part.astype(jnp.float32) * jnp.stack([gate_value, up_value], axis=1), axis=(1, 2)
    )
    act_whole = lax.all_gather(act_part[:, None, :], "head", axis=2, tiled=True)
    grad_hidden = lax.all_gather(grad_part, "head", axis=2, tiled=True)
    hidden_act = act_whole[:, 0]
    inner_sum = lax.psum(inner_part, "head")
    out_rows = jnp.dot(hidden_act, w_second, preferred_element_type=jnp.float32).astype(
        jnp.bfloat16
    )
    grad_normed = jnp.einsum(
        "rkf,dkf->rd", grad_hidden, w_first, preferred_element_type=jnp.float32
    )
    grad_rows = (
        norm_scale * grad_normed - row_float * (norm_scale * norm_scale / D) * inner_sum[:, None]
    )
    expert_out = out_rows.reshape(lead_count, item_count, width_in)
    expert_grad = grad_rows.astype(jnp.bfloat16).reshape(lead_count, item_count, width_in)
    came_out, came_grad = (
        lax.all_to_all(expert_out, "exp", split_axis=0, concat_axis=0, tiled=True),
        lax.all_to_all(expert_grad, "exp", split_axis=0, concat_axis=0, tiled=True),
    )
    picked_out = came_out.reshape(places, row_width)[place_index].reshape(
        token_count, TOP, row_width
    )
    picked_grad = came_grad.reshape(places, row_width)[place_index].reshape(
        token_count, TOP, row_width
    )
    output = attended.astype(jnp.float32) + jnp.sum(
        route_weights[:, :, None] * picked_out.astype(jnp.float32), axis=1
    )
    grad_attended = grad_out.astype(jnp.float32) + jnp.sum(
        route_weights[:, :, None] * picked_grad.astype(jnp.float32), axis=1
    )
    return (output.astype(jnp.bfloat16), grad_attended.astype(jnp.bfloat16))


def attention_kernel(head_count, group, start_ref, q_ref, k_ref, v_ref, o_ref):
    rows = q_ref.shape[0]
    cached = k_ref.shape[0]
    first = start_ref[0]
    row_pos = first + lax.broadcasted_iota(jnp.int32, (rows, cached), 0)
    visible = lax.broadcasted_iota(jnp.int32, (rows, cached), 1) <= row_pos
    for head in range(head_count):
        cols = slice(head * HEAD_WIDTH, (head + 1) * HEAD_WIDTH)
        kv_head = head // group
        kv_cols = slice(kv_head * HEAD_WIDTH, (kv_head + 1) * HEAD_WIDTH)
        scores = lax.dot_general(
            q_ref[:, cols],
            k_ref[:, kv_cols],
            (((1,), (1,)), ((), ())),
            preferred_element_type=jnp.float32,
        ) * HEAD_WIDTH ** (-0.5)
        scores = jnp.where(visible, scores, hidden_logits)
        best = jnp.max(scores, axis=1, keepdims=True)
        weights = jnp.exp(scores - best)
        total = jnp.sum(weights, axis=1, keepdims=True)
        sums = jnp.dot(
            weights.astype(jnp.bfloat16), v_ref[:, kv_cols], preferred_element_type=jnp.float32
        )
        o_ref[:, cols] = (sums / total).astype(jnp.bfloat16)


def attend_local(queries, key_all, value_all, start):
    head_count = queries.shape[1] // HEAD_WIDTH
    group = head_count // (key_all.shape[1] // HEAD_WIDTH)

    def body(*refs):
        attention_kernel(head_count, group, *refs)

    return pl.pallas_call(
        body,
        out_shape=jax.ShapeDtypeStruct(queries.shape, jnp.bfloat16),
        in_specs=[pl.BlockSpec(memory_space=pltpu.SMEM)]
        + [pl.BlockSpec(memory_space=pltpu.VMEM)] * 3,
        out_specs=pl.BlockSpec(memory_space=pltpu.VMEM),
        name="attention",
    )(start.reshape(1).astype(jnp.int32), queries, key_all, value_all)


def three_parts(value):
    high = value.astype(jnp.bfloat16)
    rest = value - high.astype(jnp.float32)
    middle = rest.astype(jnp.bfloat16)
    low = (rest - middle.astype(jnp.float32)).astype(jnp.bfloat16)
    return high, middle, low


def ring_place(index, count):
    outer, inner = index // 2, index % 2
    return outer + inner * (count - 1 - 2 * outer)


def ring_index(place, count):
    inner = place // (count // 2)
    return 2 * (place + inner * (count - 1 - 2 * place)) + inner


def ring_start(count):
    place = ring_place(lax.axis_index("exp"), count)
    right = ring_index((place + 1) % count, count)
    left = ring_index((place + count - 1) % count, count)
    barrier = pltpu.get_barrier_semaphore()
    for other in (left, right):
        pl.semaphore_signal(
            barrier, inc=1, device_id={"exp": other}, device_id_type=pl.DeviceIdType.MESH
        )
    pl.semaphore_wait(barrier, 2)
    return place, (right, left)


def ring_lanes(count):
    reach = count // 2
    return ((0, 0, reach), (1, 1, reach), (0, 1, reach - 1), (1, 0, reach - 1))


def ring_gather(count, x_ref, out_ref, send_sem, recv_sem, own_sem):
    place, others = ring_start(count)
    me = lax.axis_index("exp")
    rows = x_ref.shape[0]
    half = rows // 2
    own = pltpu.make_async_copy(
        x_ref, out_ref.at[pl.ds(pl.multiple_of(me * rows, rows), rows)], own_sem
    )
    own.start()

    def copy(way, part, step):
        shift = count - step if way == 0 else step
        owner = ring_index((place + shift) % count, count)
        spot = out_ref.at[pl.ds(pl.multiple_of(owner * rows + part * half, half), half)]
        source = x_ref.at[pl.ds(part * half, half)] if step == 0 else spot
        return pltpu.make_async_remote_copy(
            src_ref=source,
            dst_ref=spot,
            send_sem=send_sem.at[way, part, step],
            recv_sem=recv_sem.at[way, part, step],
            device_id={"exp": others[way]},
            device_id_type=pl.DeviceIdType.MESH,
        )

    copies = {}
    for step in range(count // 2):
        for way, part, steps in ring_lanes(count):
            if step < steps:
                if step > 0:
                    copies[way, part, step - 1].wait_recv()
                copies[way, part, step] = copy(way, part, step)
                copies[way, part, step].start()
    for way, part, steps in ring_lanes(count):
        copies[way, part, steps - 1].wait_recv()
    for each in copies.values():
        each.wait_send()
    own.wait()


def ring_scatter(count, x_ref, out_ref, held, send_sem, recv_sem):
    place, others = ring_start(count)
    rows = x_ref.shape[1]
    half = rows // 2

    def term(way, part, step, steps):
        shift = steps - step if way == 0 else count - steps + step
        return x_ref.at[ring_index((place + shift) % count, count), pl.ds(part * half, half)]

    copies = {}
    for step in range(count // 2):
        for way, part, steps in ring_lanes(count):
            if step < steps:
                source = term(way, part, step, steps)
                if step > 0:
                    copies[way, part, step - 1].wait_recv()
                    slot = held.at[way, step - 1, pl.ds(part * half, half)]
                    slot[...] = (
                        slot[...].astype(jnp.float32) + source[...].astype(jnp.float32)
                    ).astype(jnp.bfloat16)
                    source = slot
                copies[way, part, step] = pltpu.make_async_remote_copy(
                    src_ref=source,
                    dst_ref=held.at[way, step, pl.ds(part * half, half)],
                    send_sem=send_sem.at[way, part, step],
                    recv_sem=recv_sem.at[way, part, step],
                    device_id={"exp": others[way]},
                    device_id_type=pl.DeviceIdType.MESH,
                )
                copies[way, part, step].start()
    last = {}
    for way, part, steps in ring_lanes(count):
        copies[way, part, steps - 1].wait_recv()
        last[way, part] = steps - 1
    me = lax.axis_index("exp")
    for part in range(2):
        span = pl.ds(part * half, half)
        out_ref[span] = (
            x_ref[me, span].astype(jnp.float32)
            + held[0, last[0, part], span].astype(jnp.float32)
            + held[1, last[1, part], span].astype(jnp.float32)
        )
    for each in copies.values():
        each.wait_send()


def ring_sems(count):
    return [pltpu.SemaphoreType.DMA((2, 2, count // 2))] * 2


def gather_exp(block, tag):
    count = lax.axis_size("exp")
    rows, width = block.shape

    def gather_body(*refs):
        ring_gather(count, *refs)

    return pl.pallas_call(
        gather_body,
        out_shape=jax.ShapeDtypeStruct((count * rows, width), block.dtype),
        in_specs=[pl.BlockSpec(memory_space=pltpu.VMEM)],
        out_specs=pl.BlockSpec(memory_space=pltpu.VMEM),
        scratch_shapes=ring_sems(count) + [pltpu.SemaphoreType.DMA],
        compiler_params=pltpu.CompilerParams(collective_id=tag, has_side_effects=True),
        name="ring_gather_" + str(tag),
    )(block)


def scatter_exp(blocks, tag):
    count, rows, width = blocks.shape

    def scatter_body(*refs):
        ring_scatter(count, *refs)

    return pl.pallas_call(
        scatter_body,
        out_shape=jax.ShapeDtypeStruct((rows, width), jnp.float32),
        in_specs=[pl.BlockSpec(memory_space=pltpu.VMEM)],
        out_specs=pl.BlockSpec(memory_space=pltpu.VMEM),
        scratch_shapes=[pltpu.VMEM((2, count // 2, rows, width), blocks.dtype)]
        + ring_sems(count),
        compiler_params=pltpu.CompilerParams(collective_id=tag, has_side_effects=True),
        name="ring_scatter",
    )(blocks)


def dense_device(queries, keys, values, w_in, w_out, routes, route_weights, grad_out):
    exp_count = lax.axis_size("exp")
    exp_index = lax.axis_index("exp")
    parts = lax.axis_size("head")
    tokens, width = queries.shape
    experts = w_in.shape[0] * exp_count
    hidden = w_in.shape[3]
    share = hidden // parts
    kv_width = keys.shape[1]
    offset = keys.shape[0] * exp_count - tokens * exp_count
    w_first = w_in[0]
    w_second = w_out[0]
    hits = routes[:, :, None] == jnp.arange(experts, dtype=jnp.int32)[None, None, :]
    table = jnp.sum(jnp.where(hits, route_weights[:, :, None], 0.0), axis=1)
    packed = jnp.concatenate(three_parts(table), axis=1)
    packed = jnp.pad(packed, ((0, 0), (0, -packed.shape[1] % 128)))
    early = gather_exp(jnp.concatenate([keys, values, grad_out, packed], axis=1), 1)
    kv_all = early[:, : 2 * kv_width]
    grad_pack = early[:, 2 * kv_width :]
    grads = grad_pack[:, :width]
    attended = attend_local(
        queries, kv_all[:, :kv_width], kv_all[:, kv_width:], offset + exp_index * tokens
    )
    rows = gather_exp(attended, 2)
    count = rows.shape[0]
    pieces = grad_pack[:, width : width + 3 * experts].astype(jnp.float32)
    table_all = jnp.sum(pieces.reshape(count, 3, experts), axis=1)
    own = (jnp.arange(experts) == exp_index).astype(jnp.float32)
    gain = jnp.sum(table_all * own[None, :], axis=1)[:, None]
    w_split = w_first.reshape(width, 2, parts, share)
    second_split = w_second.reshape(parts, share, width)
    back_sums = jnp.einsum(
        "rd,hfd->hrf", grads, second_split, preferred_element_type=jnp.float32
    ).astype(jnp.bfloat16)
    back_value = lax.psum_scatter(back_sums, "head", scatter_dimension=0, tiled=False)
    row_float = rows.astype(jnp.float32)
    raw_sums = jnp.einsum("rd,dkhf->hrkf", rows, w_split, preferred_element_type=jnp.float32)
    raw_sums = raw_sums.astype(jnp.bfloat16).reshape(parts, count, 2 * share)
    squares = jnp.sum(row_float * row_float, axis=1)
    square_tile = jnp.broadcast_to(
        squares.astype(jnp.bfloat16)[None, :, None], (parts, count, 128)
    )
    raw_part = lax.psum_scatter(
        jnp.concatenate([raw_sums, square_tile], axis=2),
        "head",
        scatter_dimension=0,
        tiled=False,
    ).astype(jnp.float32)
    norm_scale = lax.rsqrt(raw_part[:, 2 * share : 2 * share + 1] / D + norm_eps)
    gate_value = raw_part[:, :share] * norm_scale
    up_value = raw_part[:, share : 2 * share] * norm_scale
    back_value = back_value.astype(jnp.float32)
    sigmoid = jax.nn.sigmoid(gate_value)
    silu = gate_value * sigmoid
    act = (silu * up_value).astype(jnp.bfloat16)
    grad_gate = (back_value * up_value * sigmoid * (1.0 + gate_value * (1.0 - sigmoid))).astype(
        jnp.bfloat16
    )
    grad_up = (back_value * silu).astype(jnp.bfloat16)
    inner = jnp.sum(
        grad_gate.astype(jnp.float32) * gate_value + grad_up.astype(jnp.float32) * up_value,
        axis=1,
        keepdims=True,
    )
    sent = jnp.concatenate([act, grad_gate, grad_up, *three_parts(inner)], axis=1)
    sent = jnp.pad(sent, ((0, 0), (0, -sent.shape[1] % 128)))
    whole = lax.all_gather(sent, "head", axis=0, tiled=False)
    inner_sum = jnp.sum(whole[:, :, 3 * share : 3 * share + 3].astype(jnp.float32), axis=(0, 2))[
        :, None
    ]
    act_all = jnp.transpose(whole[:, :, :share], (1, 0, 2)).reshape(count, hidden)
    gate_all = jnp.transpose(whole[:, :, share : 2 * share], (1, 0, 2)).reshape(count, hidden)
    up_all = jnp.transpose(whole[:, :, 2 * share : 3 * share], (1, 0, 2)).reshape(count, hidden)
    grad_all = jnp.concatenate([gate_all, up_all], axis=1)
    out_rows = jnp.dot(act_all, w_second, preferred_element_type=jnp.float32)
    grad_normed = lax.dot_general(
        grad_all,
        w_first.reshape(width, 2 * hidden),
        (((1,), (1,)), ((), ())),
        preferred_element_type=jnp.float32,
    )
    grad_rows = norm_scale * grad_normed - row_float * (norm_scale * norm_scale / D) * inner_sum
    routed = gain > 0.0
    both = jnp.concatenate(
        [
            jnp.where(routed, gain * out_rows, 0.0).astype(jnp.bfloat16),
            jnp.where(routed, gain * grad_rows, 0.0).astype(jnp.bfloat16),
        ],
        axis=1,
    )
    summed = scatter_exp(both.reshape(exp_count, tokens, 2 * width), 3)
    output = attended.astype(jnp.float32) + summed[:, :width]
    grad_attended = grad_out.astype(jnp.float32) + summed[:, width:]
    return (output.astype(jnp.bfloat16), grad_attended.astype(jnp.bfloat16))


def solution(mesh):
    dense = 2 * TOP >= mesh.shape["exp"] and mesh.shape["exp"] % 2 == 0
    in_specs = (
        P("exp", "head"),
        P("exp", "head"),
        P("exp", "head"),
        P("exp", "head", None, None),
        P("exp", None, "head"),
        P("exp", None),
        P("exp", None),
        P("exp", "head"),
    )
    out_specs = (P("exp", "head"), P("exp", "head"))
    return jax.shard_map(
        dense_device if dense else per_device, mesh=mesh, in_specs=in_specs, out_specs=out_specs, check_vma=False
    )
```

```python
import jax
import jax.numpy as jnp
from jax import lax
from jax.experimental import pallas as pl
from jax.experimental.pallas import tpu as pltpu
from jax.sharding import PartitionSpec as P

D = 4096
HEAD_WIDTH = 128
TOP = 6


norm_eps = 1e-05
hidden_logits = -1e30


def block_partial(query_rows, query_pos, rows_of_keys, value_rows, key_pos):
    row_count = query_rows.shape[0]
    count_of_blocks = rows_of_keys.shape[0]
    kv_heads = rows_of_keys.shape[2] // HEAD_WIDTH
    grouping_width = query_rows.shape[1] // HEAD_WIDTH // kv_heads
    heads_of_queries = query_rows.reshape(row_count, kv_heads, grouping_width, HEAD_WIDTH)
    key_heads = rows_of_keys.reshape(count_of_blocks, -1, kv_heads, HEAD_WIDTH)
    value_heads = value_rows.reshape(count_of_blocks, -1, kv_heads, HEAD_WIDTH)
    visible = (key_pos[:, None, :] <= query_pos[None, :, None])[:, :, None, None, :]
    scores = jnp.einsum(
        "tgid,bjgd->btgij", heads_of_queries, key_heads, preferred_element_type=jnp.float32
    ) * HEAD_WIDTH ** (-0.5)
    scores = jnp.where(visible, scores, hidden_logits)
    best_score = jnp.max(scores, axis=-1).astype(jnp.bfloat16)
    weights = jnp.where(visible, jnp.exp(scores - best_score.astype(jnp.float32)[..., None]), 0.0)
    weight_total = jnp.sum(weights, axis=-1).astype(jnp.bfloat16)
    weighted_sum = jnp.einsum(
        "btgij,bjgd->btgid",
        weights.astype(jnp.bfloat16),
        value_heads,
        preferred_element_type=jnp.float32,
    ).astype(jnp.bfloat16)
    head_count = kv_heads * grouping_width
    return (
        best_score.reshape(count_of_blocks, row_count, head_count),
        weight_total.reshape(count_of_blocks, row_count, head_count),
        weighted_sum.reshape(count_of_blocks, row_count, head_count * HEAD_WIDTH),
    )


def fold_partials(running, best_score, weight_total, weighted_sum):
    top_now, total_now, sums_now = running
    best_value = best_score.astype(jnp.float32)
    new_top = jnp.maximum(top_now, jnp.max(best_value, axis=0))
    old_factor = jnp.exp(top_now - new_top)
    block_factor = jnp.exp(best_value - new_top[None])
    total_next = total_now * old_factor + jnp.sum(
        weight_total.astype(jnp.float32) * block_factor, axis=0
    )
    spread_sums = weighted_sum.reshape(
        weighted_sum.shape[0], sums_now.shape[0], sums_now.shape[1], HEAD_WIDTH
    )
    sums_next = sums_now * old_factor[..., None] + jnp.sum(
        spread_sums.astype(jnp.float32) * block_factor[..., None], axis=0
    )
    return (new_top, total_next, sums_next)


def per_device(queries, keys, values, w_in, w_out, routes, route_weights, grad_out):
    exp_count = lax.axis_size("exp")
    exp_index = lax.axis_index("exp")
    head_devices = lax.axis_size("head")
    token_count = queries.shape[0]
    query_width = queries.shape[1]
    head_count = query_width // HEAD_WIDTH
    cache_rows = keys.shape[0]
    window = token_count * exp_count
    offset = cache_rows * exp_count - window
    beginning = (
        jnp.full((token_count, head_count), hidden_logits, jnp.float32),
        jnp.zeros((token_count, head_count), jnp.float32),
        jnp.zeros((token_count, head_count, HEAD_WIDTH), jnp.float32),
    )
    own_pos = offset + exp_index * token_count + jnp.arange(token_count, dtype=jnp.int32)
    key_piece = lax.all_gather(keys, "exp", axis=0, tiled=True)
    value_piece = lax.all_gather(values, "exp", axis=0, tiled=True)
    piece_blocks = key_piece.shape[0] // cache_rows
    key_split = key_piece.reshape(piece_blocks, cache_rows, -1)
    value_split = value_piece.reshape(piece_blocks, cache_rows, -1)
    pos_split = jnp.arange(key_piece.shape[0], dtype=jnp.int32).reshape(piece_blocks, cache_rows)

    def one_block(state, element):
        key_block, value_block, pos_block = element
        block_parts = block_partial(
            queries, own_pos, key_block[None], value_block[None], pos_block[None]
        )
        return (fold_partials(state, block_parts[0], block_parts[1], block_parts[2]), None)

    state, ignored = lax.scan(one_block, beginning, (key_split, value_split, pos_split))
    attended = (
        (state[2] / state[1][..., None]).reshape(token_count, query_width).astype(jnp.bfloat16)
    )
    row_width = attended.shape[1]
    experts_all = w_in.shape[0] * exp_count
    mean_load = TOP * token_count // experts_all
    capacity = mean_load + mean_load // 6
    places = experts_all * capacity
    flat_routes = routes.reshape(-1)
    expert_hits = (
        flat_routes[:, None] == jnp.arange(experts_all, dtype=jnp.int32)[None, :]
    ).astype(jnp.int32)
    earlier = jnp.cumsum(expert_hits, axis=0) - expert_hits
    slot_index = jnp.sum(earlier * expert_hits, axis=1)
    place_index = flat_routes * capacity + slot_index
    chosen = (place_index[:, None] == jnp.arange(places, dtype=jnp.int32)[None, :]).astype(
        jnp.bfloat16
    )
    picker = jnp.sum(chosen.reshape(token_count, TOP, places), axis=1)
    contract_rows = (((0,), (0,)), ((), ()))
    send_rows = lax.dot_general(picker, attended, contract_rows, preferred_element_type=jnp.float32)
    send_rows = send_rows.astype(jnp.bfloat16).reshape(experts_all, capacity, row_width)
    send_grads = lax.dot_general(
        picker, grad_out, contract_rows, preferred_element_type=jnp.float32
    )
    send_grads = send_grads.astype(jnp.bfloat16).reshape(experts_all, capacity, row_width)
    w_first = w_in[0]
    w_second = w_out[0]
    rows_in = lax.all_to_all(send_rows, "exp", split_axis=0, concat_axis=0, tiled=True)
    grads_in = lax.all_to_all(send_grads, "exp", split_axis=0, concat_axis=0, tiled=True)
    lead_count, item_count, width_in = rows_in.shape
    row_total = lead_count * item_count
    row_block = rows_in.reshape(row_total, width_in)
    grad_block = grads_in.reshape(row_total, width_in)
    row_float = row_block.astype(jnp.float32)
    raw_sums = jnp.einsum("rd,dkf->rkf", row_block, w_first, preferred_element_type=jnp.float32)
    back_sums = lax.dot_general(
        grad_block, w_second, (((1,), (1,)), ((), ())), preferred_element_type=jnp.float32
    )
    squares = jnp.sum(row_float * row_float, axis=1)
    square_tile = jnp.broadcast_to(squares[:, None, None], (row_total, 1, head_devices))
    raw_part = lax.psum_scatter(raw_sums, "head", scatter_dimension=2, tiled=True)
    back_part = lax.psum_scatter(back_sums[:, None, :], "head", scatter_dimension=2, tiled=True)
    square_part = lax.psum_scatter(square_tile, "head", scatter_dimension=2, tiled=True)
    norm_scale = lax.rsqrt(square_part[:, 0] / D + norm_eps)
    gate_value = raw_part[:, 0] * norm_scale
    up_value = raw_part[:, 1] * norm_scale
    back_value = back_part[:, 0]
    gate_sigmoid = jax.nn.sigmoid(gate_value)
    gate_silu = gate_value * gate_sigmoid
    act_part = (gate_silu * up_value).astype(jnp.bfloat16)
    grad_gate = back_value * up_value * gate_sigmoid * (1.0 + gate_value * (1.0 - gate_sigmoid))
    grad_up = back_value * gate_silu
    grad_part = jnp.stack([grad_gate, grad_up], axis=1).astype(jnp.bfloat16)
    inner_part = jnp.sum(
        grad_part.astype(jnp.float32) * jnp.stack([gate_value, up_value], axis=1), axis=(1, 2)
    )
    act_whole = lax.all_gather(act_part[:, None, :], "head", axis=2, tiled=True)
    grad_hidden = lax.all_gather(grad_part, "head", axis=2, tiled=True)
    hidden_act = act_whole[:, 0]
    inner_sum = lax.psum(inner_part, "head")
    out_rows = jnp.dot(hidden_act, w_second, preferred_element_type=jnp.float32).astype(
        jnp.bfloat16
    )
    grad_normed = jnp.einsum(
        "rkf,dkf->rd", grad_hidden, w_first, preferred_element_type=jnp.float32
    )
    grad_rows = (
        norm_scale * grad_normed - row_float * (norm_scale * norm_scale / D) * inner_sum[:, None]
    )
    expert_out = out_rows.reshape(lead_count, item_count, width_in)
    expert_grad = grad_rows.astype(jnp.bfloat16).reshape(lead_count, item_count, width_in)
    came_out, came_grad = (
        lax.all_to_all(expert_out, "exp", split_axis=0, concat_axis=0, tiled=True),
        lax.all_to_all(expert_grad, "exp", split_axis=0, concat_axis=0, tiled=True),
    )
    picked_out = came_out.reshape(places, row_width)[place_index].reshape(
        token_count, TOP, row_width
    )
    picked_grad = came_grad.reshape(places, row_width)[place_index].reshape(
        token_count, TOP, row_width
    )
    output = attended.astype(jnp.float32) + jnp.sum(
        route_weights[:, :, None] * picked_out.astype(jnp.float32), axis=1
    )
    grad_attended = grad_out.astype(jnp.float32) + jnp.sum(
        route_weights[:, :, None] * picked_grad.astype(jnp.float32), axis=1
    )
    return (output.astype(jnp.bfloat16), grad_attended.astype(jnp.bfloat16))


def attention_kernel(head_count, group, start_ref, q_ref, k_ref, v_ref, o_ref):
    rows = q_ref.shape[0]
    cached = k_ref.shape[0]
    first = start_ref[0]
    row_pos = first + lax.broadcasted_iota(jnp.int32, (rows, cached), 0)
    visible = lax.broadcasted_iota(jnp.int32, (rows, cached), 1) <= row_pos
    for head in range(head_count):
        cols = slice(head * HEAD_WIDTH, (head + 1) * HEAD_WIDTH)
        kv_head = head // group
        kv_cols = slice(kv_head * HEAD_WIDTH, (kv_head + 1) * HEAD_WIDTH)
        scores = lax.dot_general(
            q_ref[:, cols],
            k_ref[:, kv_cols],
            (((1,), (1,)), ((), ())),
            preferred_element_type=jnp.float32,
        ) * HEAD_WIDTH ** (-0.5)
        scores = jnp.where(visible, scores, hidden_logits)
        best = jnp.max(scores, axis=1, keepdims=True)
        weights = jnp.exp(scores - best)
        total = jnp.sum(weights, axis=1, keepdims=True)
        sums = jnp.dot(
            weights.astype(jnp.bfloat16), v_ref[:, kv_cols], preferred_element_type=jnp.float32
        )
        o_ref[:, cols] = (sums / total).astype(jnp.bfloat16)


def attend_local(queries, key_all, value_all, start):
    head_count = queries.shape[1] // HEAD_WIDTH
    group = head_count // (key_all.shape[1] // HEAD_WIDTH)

    def body(*refs):
        attention_kernel(head_count, group, *refs)

    return pl.pallas_call(
        body,
        out_shape=jax.ShapeDtypeStruct(queries.shape, jnp.bfloat16),
        in_specs=[pl.BlockSpec(memory_space=pltpu.SMEM)]
        + [pl.BlockSpec(memory_space=pltpu.VMEM)] * 3,
        out_specs=pl.BlockSpec(memory_space=pltpu.VMEM),
        name="attention",
    )(start.reshape(1).astype(jnp.int32), queries, key_all, value_all)


def three_parts(value):
    high = value.astype(jnp.bfloat16)
    rest = value - high.astype(jnp.float32)
    middle = rest.astype(jnp.bfloat16)
    low = (rest - middle.astype(jnp.float32)).astype(jnp.bfloat16)
    return high, middle, low


def ring_place(index, count):
    outer, inner = index // 2, index % 2
    return outer + inner * (count - 1 - 2 * outer)


def ring_index(place, count):
    inner = place // (count // 2)
    return 2 * (place + inner * (count - 1 - 2 * place)) + inner


def ring_start(count):
    place = ring_place(lax.axis_index("exp"), count)
    right = ring_index((place + 1) % count, count)
    left = ring_index((place + count - 1) % count, count)
    barrier = pltpu.get_barrier_semaphore()
    for other in (left, right):
        pl.semaphore_signal(
            barrier, inc=1, device_id={"exp": other}, device_id_type=pl.DeviceIdType.MESH
        )
    pl.semaphore_wait(barrier, 2)
    return place, (right, left)


def ring_lanes(count):
    reach = count // 2
    return ((0, 0, reach), (1, 1, reach), (0, 1, reach - 1), (1, 0, reach - 1))


def ring_gather(count, x_ref, out_ref, send_sem, recv_sem, own_sem):
    place, others = ring_start(count)
    me = lax.axis_index("exp")
    rows = x_ref.shape[0]
    half = rows // 2
    own = pltpu.make_async_copy(
        x_ref, out_ref.at[pl.ds(pl.multiple_of(me * rows, rows), rows)], own_sem
    )
    own.start()

    def copy(way, part, step):
        shift = count - step if way == 0 else step
        owner = ring_index((place + shift) % count, count)
        spot = out_ref.at[pl.ds(pl.multiple_of(owner * rows + part * half, half), half)]
        source = x_ref.at[pl.ds(part * half, half)] if step == 0 else spot
        return pltpu.make_async_remote_copy(
            src_ref=source,
            dst_ref=spot,
            send_sem=send_sem.at[way, part, step],
            recv_sem=recv_sem.at[way, part, step],
            device_id={"exp": others[way]},
            device_id_type=pl.DeviceIdType.MESH,
        )

    copies = {}
    for step in range(count // 2):
        for way, part, steps in ring_lanes(count):
            if step < steps:
                if step > 0:
                    copies[way, part, step - 1].wait_recv()
                copies[way, part, step] = copy(way, part, step)
                copies[way, part, step].start()
    for way, part, steps in ring_lanes(count):
        copies[way, part, steps - 1].wait_recv()
    for each in copies.values():
        each.wait_send()
    own.wait()


def ring_scatter(count, x_ref, out_ref, held, send_sem, recv_sem):
    place, others = ring_start(count)
    rows = x_ref.shape[1]
    half = rows // 2

    def term(way, part, step, steps):
        shift = steps - step if way == 0 else count - steps + step
        return x_ref.at[ring_index((place + shift) % count, count), pl.ds(part * half, half)]

    copies = {}
    for step in range(count // 2):
        for way, part, steps in ring_lanes(count):
            if step < steps:
                source = term(way, part, step, steps)
                if step > 0:
                    copies[way, part, step - 1].wait_recv()
                    slot = held.at[way, step - 1, pl.ds(part * half, half)]
                    slot[...] = (
                        slot[...].astype(jnp.float32) + source[...].astype(jnp.float32)
                    ).astype(jnp.bfloat16)
                    source = slot
                copies[way, part, step] = pltpu.make_async_remote_copy(
                    src_ref=source,
                    dst_ref=held.at[way, step, pl.ds(part * half, half)],
                    send_sem=send_sem.at[way, part, step],
                    recv_sem=recv_sem.at[way, part, step],
                    device_id={"exp": others[way]},
                    device_id_type=pl.DeviceIdType.MESH,
                )
                copies[way, part, step].start()
    last = {}
    for way, part, steps in ring_lanes(count):
        copies[way, part, steps - 1].wait_recv()
        last[way, part] = steps - 1
    me = lax.axis_index("exp")
    for part in range(2):
        span = pl.ds(part * half, half)
        out_ref[span] = (
            x_ref[me, span].astype(jnp.float32)
            + held[0, last[0, part], span].astype(jnp.float32)
            + held[1, last[1, part], span].astype(jnp.float32)
        )
    for each in copies.values():
        each.wait_send()


def ring_sems(count):
    return [pltpu.SemaphoreType.DMA((2, 2, count // 2))] * 2


def gather_exp(block, tag):
    count = lax.axis_size("exp")
    rows, width = block.shape

    def gather_body(*refs):
        ring_gather(count, *refs)

    return pl.pallas_call(
        gather_body,
        out_shape=jax.ShapeDtypeStruct((count * rows, width), block.dtype),
        in_specs=[pl.BlockSpec(memory_space=pltpu.VMEM)],
        out_specs=pl.BlockSpec(memory_space=pltpu.VMEM),
        scratch_shapes=ring_sems(count) + [pltpu.SemaphoreType.DMA],
        compiler_params=pltpu.CompilerParams(collective_id=tag, has_side_effects=True),
        name="ring_gather_" + str(tag),
    )(block)


def scatter_exp(blocks, tag):
    count, rows, width = blocks.shape

    def scatter_body(*refs):
        ring_scatter(count, *refs)

    return pl.pallas_call(
        scatter_body,
        out_shape=jax.ShapeDtypeStruct((rows, width), jnp.float32),
        in_specs=[pl.BlockSpec(memory_space=pltpu.VMEM)],
        out_specs=pl.BlockSpec(memory_space=pltpu.VMEM),
        scratch_shapes=[pltpu.VMEM((2, count // 2, rows, width), blocks.dtype)]
        + ring_sems(count),
        compiler_params=pltpu.CompilerParams(collective_id=tag, has_side_effects=True),
        name="ring_scatter",
    )(blocks)


def pair_start():
    me = lax.axis_index("head")
    mate = me + 1 - 2 * (me % 2)
    across = (me + 2) % 4
    barrier = pltpu.get_barrier_semaphore()
    for other in (mate, across):
        pl.semaphore_signal(
            barrier, inc=1, device_id={"head": other}, device_id_type=pl.DeviceIdType.MESH
        )
    pl.semaphore_wait(barrier, 2)
    return me, mate, across


def pair_copy(source, target, send_sem, recv_sem, other):
    copy = pltpu.make_async_remote_copy(
        src_ref=source,
        dst_ref=target,
        send_sem=send_sem,
        recv_sem=recv_sem,
        device_id={"head": other},
        device_id_type=pl.DeviceIdType.MESH,
    )
    copy.start()
    return copy


def pair_scatter(chunks, x_ref, out_ref, near, far, send_sem, recv_sem):
    me, mate, across = pair_start()
    step = x_ref.shape[1] // chunks
    spans = [pl.ds(part * step, step) for part in range(chunks)]
    copies = {}
    for kind, dest in ((0, (mate + 2) % 4), (1, mate)):
        for part, span in enumerate(spans):
            copies[kind, part] = pair_copy(
                x_ref.at[dest, span],
                near.at[kind, span],
                send_sem.at[kind, part],
                recv_sem.at[kind, part],
                mate,
            )
    for part, span in enumerate(spans):
        copies[0, part].wait_recv()
        near[0, span] = (
            near[0, span].astype(jnp.float32) + x_ref[across, span].astype(jnp.float32)
        ).astype(jnp.bfloat16)
        copies[2, part] = pair_copy(
            near.at[0, span], far.at[span], send_sem.at[2, part], recv_sem.at[2, part], across
        )
    for part, span in enumerate(spans):
        copies[1, part].wait_recv()
        copies[2, part].wait_recv()
        out_ref[span] = (
            x_ref[me, span].astype(jnp.float32)
            + near[1, span].astype(jnp.float32)
            + far[span].astype(jnp.float32)
        )
    for each in copies.values():
        each.wait_send()


def pair_gather(chunks, x_ref, out_ref, send_sem, recv_sem, own_sem):
    me, mate, across = pair_start()
    own = pltpu.make_async_copy(x_ref, out_ref.at[me], own_sem)
    own.start()
    step = x_ref.shape[0] // chunks
    spans = [pl.ds(part * step, step) for part in range(chunks)]
    copies = {}
    for kind, other in ((0, across), (1, mate)):
        for part, span in enumerate(spans):
            copies[kind, part] = pair_copy(
                x_ref.at[span],
                out_ref.at[me, span],
                send_sem.at[kind, part],
                recv_sem.at[kind, part],
                other,
            )
    for part, span in enumerate(spans):
        copies[0, part].wait_recv()
        copies[2, part] = pair_copy(
            out_ref.at[across, span],
            out_ref.at[across, span],
            send_sem.at[2, part],
            recv_sem.at[2, part],
            mate,
        )
    for part in range(chunks):
        copies[1, part].wait_recv()
        copies[2, part].wait_recv()
    for each in copies.values():
        each.wait_send()
    own.wait()


def pair_sems(chunks):
    return [pltpu.SemaphoreType.DMA((3, chunks))] * 2


def scatter_head(blocks, tag):
    parts, rows, width = blocks.shape

    def body(*refs):
        pair_scatter(8, *refs)

    return pl.pallas_call(
        body,
        out_shape=jax.ShapeDtypeStruct((rows, width), jnp.float32),
        in_specs=[pl.BlockSpec(memory_space=pltpu.VMEM)],
        out_specs=pl.BlockSpec(memory_space=pltpu.VMEM),
        scratch_shapes=[
            pltpu.VMEM((2, rows, width), blocks.dtype),
            pltpu.VMEM((rows, width), blocks.dtype),
        ]
        + pair_sems(8),
        compiler_params=pltpu.CompilerParams(collective_id=tag, has_side_effects=True),
        name="pair_scatter",
    )(blocks)


def gather_head(block, tag):
    def body(*refs):
        pair_gather(8, *refs)

    return pl.pallas_call(
        body,
        out_shape=jax.ShapeDtypeStruct((4,) + block.shape, block.dtype),
        in_specs=[pl.BlockSpec(memory_space=pltpu.VMEM)],
        out_specs=pl.BlockSpec(memory_space=pltpu.VMEM),
        scratch_shapes=pair_sems(8) + [pltpu.SemaphoreType.DMA],
        compiler_params=pltpu.CompilerParams(collective_id=tag, has_side_effects=True),
        name="pair_gather",
    )(block)


def dense_device(queries, keys, values, w_in, w_out, routes, route_weights, grad_out):
    exp_count = lax.axis_size("exp")
    exp_index = lax.axis_index("exp")
    parts = lax.axis_size("head")
    tokens, width = queries.shape
    experts = w_in.shape[0] * exp_count
    hidden = w_in.shape[3]
    share = hidden // parts
    kv_width = keys.shape[1]
    offset = keys.shape[0] * exp_count - tokens * exp_count
    w_first = w_in[0]
    w_second = w_out[0]
    hits = routes[:, :, None] == jnp.arange(experts, dtype=jnp.int32)[None, None, :]
    table = jnp.sum(jnp.where(hits, route_weights[:, :, None], 0.0), axis=1)
    packed = jnp.concatenate(three_parts(table), axis=1)
    packed = jnp.pad(packed, ((0, 0), (0, -packed.shape[1] % 128)))
    early = gather_exp(jnp.concatenate([keys, values, grad_out, packed], axis=1), 1)
    kv_all = early[:, : 2 * kv_width]
    grad_pack = early[:, 2 * kv_width :]
    grads = grad_pack[:, :width]
    attended = attend_local(
        queries, kv_all[:, :kv_width], kv_all[:, kv_width:], offset + exp_index * tokens
    )
    rows = gather_exp(attended, 2)
    count = rows.shape[0]
    pieces = grad_pack[:, width : width + 3 * experts].astype(jnp.float32)
    table_all = jnp.sum(pieces.reshape(count, 3, experts), axis=1)
    own = (jnp.arange(experts) == exp_index).astype(jnp.float32)
    gain = jnp.sum(table_all * own[None, :], axis=1)[:, None]
    w_split = w_first.reshape(width, 2, parts, share)
    second_split = w_second.reshape(parts, share, width)
    back_sums = jnp.einsum(
        "rd,hfd->hrf", grads, second_split, preferred_element_type=jnp.float32
    ).astype(jnp.bfloat16)
    row_float = rows.astype(jnp.float32)
    raw_sums = jnp.einsum("rd,dkhf->hrkf", rows, w_split, preferred_element_type=jnp.float32)
    raw_sums = raw_sums.astype(jnp.bfloat16).reshape(parts, count, 2 * share)
    squares = jnp.sum(row_float * row_float, axis=1)
    square_tile = jnp.broadcast_to(
        squares.astype(jnp.bfloat16)[None, :, None], (parts, count, -3 * share % 128 + 128 * (share * 3 % 128 == 0))
    )
    raw_part = scatter_head(jnp.concatenate([raw_sums, back_sums, square_tile], axis=2), 4)
    norm_scale = lax.rsqrt(raw_part[:, 3 * share : 3 * share + 1] / D + norm_eps)
    gate_value = raw_part[:, :share] * norm_scale
    up_value = raw_part[:, share : 2 * share] * norm_scale
    back_value = raw_part[:, 2 * share : 3 * share]
    sigmoid = jax.nn.sigmoid(gate_value)
    silu = gate_value * sigmoid
    act = (silu * up_value).astype(jnp.bfloat16)
    grad_gate = (back_value * up_value * sigmoid * (1.0 + gate_value * (1.0 - sigmoid))).astype(
        jnp.bfloat16
    )
    grad_up = (back_value * silu).astype(jnp.bfloat16)
    inner = jnp.sum(
        grad_gate.astype(jnp.float32) * gate_value + grad_up.astype(jnp.float32) * up_value,
        axis=1,
        keepdims=True,
    )
    sent = jnp.concatenate([act, grad_gate, grad_up, *three_parts(inner)], axis=1)
    sent = jnp.pad(sent, ((0, 0), (0, -sent.shape[1] % 128)))
    whole = gather_head(sent, 5)
    inner_sum = jnp.sum(whole[:, :, 3 * share : 3 * share + 3].astype(jnp.float32), axis=(0, 2))[
        :, None
    ]
    act_all = jnp.transpose(whole[:, :, :share], (1, 0, 2)).reshape(count, hidden)
    gate_all = jnp.transpose(whole[:, :, share : 2 * share], (1, 0, 2)).reshape(count, hidden)
    up_all = jnp.transpose(whole[:, :, 2 * share : 3 * share], (1, 0, 2)).reshape(count, hidden)
    grad_all = jnp.concatenate([gate_all, up_all], axis=1)
    out_rows = jnp.dot(act_all, w_second, preferred_element_type=jnp.float32)
    grad_normed = lax.dot_general(
        grad_all,
        w_first.reshape(width, 2 * hidden),
        (((1,), (1,)), ((), ())),
        preferred_element_type=jnp.float32,
    )
    grad_rows = norm_scale * grad_normed - row_float * (norm_scale * norm_scale / D) * inner_sum
    routed = gain > 0.0
    both = jnp.concatenate(
        [
            jnp.where(routed, gain * out_rows, 0.0).astype(jnp.bfloat16),
            jnp.where(routed, gain * grad_rows, 0.0).astype(jnp.bfloat16),
        ],
        axis=1,
    )
    summed = scatter_exp(both.reshape(exp_count, tokens, 2 * width), 3)
    output = attended.astype(jnp.float32) + summed[:, :width]
    grad_attended = grad_out.astype(jnp.float32) + summed[:, width:]
    return (output.astype(jnp.bfloat16), grad_attended.astype(jnp.bfloat16))


def solution(mesh):
    dense = 2 * TOP >= mesh.shape["exp"] and mesh.shape["exp"] % 2 == 0 and mesh.shape["head"] == 4
    in_specs = (
        P("exp", "head"),
        P("exp", "head"),
        P("exp", "head"),
        P("exp", "head", None, None),
        P("exp", None, "head"),
        P("exp", None),
        P("exp", None),
        P("exp", "head"),
    )
    out_specs = (P("exp", "head"), P("exp", "head"))
    return jax.shard_map(
        dense_device if dense else per_device, mesh=mesh, in_specs=in_specs, out_specs=out_specs, check_vma=False
    )
```

```python
import jax
import jax.numpy as jnp
from jax import lax
from jax.experimental import pallas as pl
from jax.experimental.pallas import tpu as pltpu
from jax.sharding import PartitionSpec as P

D = 4096
HEAD_WIDTH = 128
TOP = 6


norm_eps = 1e-05
hidden_logits = -1e30


def block_partial(query_rows, query_pos, rows_of_keys, value_rows, key_pos):
    row_count = query_rows.shape[0]
    count_of_blocks = rows_of_keys.shape[0]
    kv_heads = rows_of_keys.shape[2] // HEAD_WIDTH
    grouping_width = query_rows.shape[1] // HEAD_WIDTH // kv_heads
    heads_of_queries = query_rows.reshape(row_count, kv_heads, grouping_width, HEAD_WIDTH)
    key_heads = rows_of_keys.reshape(count_of_blocks, -1, kv_heads, HEAD_WIDTH)
    value_heads = value_rows.reshape(count_of_blocks, -1, kv_heads, HEAD_WIDTH)
    visible = (key_pos[:, None, :] <= query_pos[None, :, None])[:, :, None, None, :]
    scores = jnp.einsum(
        "tgid,bjgd->btgij", heads_of_queries, key_heads, preferred_element_type=jnp.float32
    ) * HEAD_WIDTH ** (-0.5)
    scores = jnp.where(visible, scores, hidden_logits)
    best_score = jnp.max(scores, axis=-1).astype(jnp.bfloat16)
    weights = jnp.where(visible, jnp.exp(scores - best_score.astype(jnp.float32)[..., None]), 0.0)
    weight_total = jnp.sum(weights, axis=-1).astype(jnp.bfloat16)
    weighted_sum = jnp.einsum(
        "btgij,bjgd->btgid",
        weights.astype(jnp.bfloat16),
        value_heads,
        preferred_element_type=jnp.float32,
    ).astype(jnp.bfloat16)
    head_count = kv_heads * grouping_width
    return (
        best_score.reshape(count_of_blocks, row_count, head_count),
        weight_total.reshape(count_of_blocks, row_count, head_count),
        weighted_sum.reshape(count_of_blocks, row_count, head_count * HEAD_WIDTH),
    )


def fold_partials(running, best_score, weight_total, weighted_sum):
    top_now, total_now, sums_now = running
    best_value = best_score.astype(jnp.float32)
    new_top = jnp.maximum(top_now, jnp.max(best_value, axis=0))
    old_factor = jnp.exp(top_now - new_top)
    block_factor = jnp.exp(best_value - new_top[None])
    total_next = total_now * old_factor + jnp.sum(
        weight_total.astype(jnp.float32) * block_factor, axis=0
    )
    spread_sums = weighted_sum.reshape(
        weighted_sum.shape[0], sums_now.shape[0], sums_now.shape[1], HEAD_WIDTH
    )
    sums_next = sums_now * old_factor[..., None] + jnp.sum(
        spread_sums.astype(jnp.float32) * block_factor[..., None], axis=0
    )
    return (new_top, total_next, sums_next)


def per_device(queries, keys, values, w_in, w_out, routes, route_weights, grad_out):
    exp_count = lax.axis_size("exp")
    exp_index = lax.axis_index("exp")
    head_devices = lax.axis_size("head")
    token_count = queries.shape[0]
    query_width = queries.shape[1]
    head_count = query_width // HEAD_WIDTH
    cache_rows = keys.shape[0]
    window = token_count * exp_count
    offset = cache_rows * exp_count - window
    beginning = (
        jnp.full((token_count, head_count), hidden_logits, jnp.float32),
        jnp.zeros((token_count, head_count), jnp.float32),
        jnp.zeros((token_count, head_count, HEAD_WIDTH), jnp.float32),
    )
    own_pos = offset + exp_index * token_count + jnp.arange(token_count, dtype=jnp.int32)
    key_piece = lax.all_gather(keys, "exp", axis=0, tiled=True)
    value_piece = lax.all_gather(values, "exp", axis=0, tiled=True)
    piece_blocks = key_piece.shape[0] // cache_rows
    key_split = key_piece.reshape(piece_blocks, cache_rows, -1)
    value_split = value_piece.reshape(piece_blocks, cache_rows, -1)
    pos_split = jnp.arange(key_piece.shape[0], dtype=jnp.int32).reshape(piece_blocks, cache_rows)

    def one_block(state, element):
        key_block, value_block, pos_block = element
        block_parts = block_partial(
            queries, own_pos, key_block[None], value_block[None], pos_block[None]
        )
        return (fold_partials(state, block_parts[0], block_parts[1], block_parts[2]), None)

    state, ignored = lax.scan(one_block, beginning, (key_split, value_split, pos_split))
    attended = (
        (state[2] / state[1][..., None]).reshape(token_count, query_width).astype(jnp.bfloat16)
    )
    row_width = attended.shape[1]
    experts_all = w_in.shape[0] * exp_count
    mean_load = TOP * token_count // experts_all
    capacity = mean_load + mean_load // 6
    places = experts_all * capacity
    flat_routes = routes.reshape(-1)
    expert_hits = (
        flat_routes[:, None] == jnp.arange(experts_all, dtype=jnp.int32)[None, :]
    ).astype(jnp.int32)
    earlier = jnp.cumsum(expert_hits, axis=0) - expert_hits
    slot_index = jnp.sum(earlier * expert_hits, axis=1)
    place_index = flat_routes * capacity + slot_index
    chosen = (place_index[:, None] == jnp.arange(places, dtype=jnp.int32)[None, :]).astype(
        jnp.bfloat16
    )
    picker = jnp.sum(chosen.reshape(token_count, TOP, places), axis=1)
    contract_rows = (((0,), (0,)), ((), ()))
    send_rows = lax.dot_general(picker, attended, contract_rows, preferred_element_type=jnp.float32)
    send_rows = send_rows.astype(jnp.bfloat16).reshape(experts_all, capacity, row_width)
    send_grads = lax.dot_general(
        picker, grad_out, contract_rows, preferred_element_type=jnp.float32
    )
    send_grads = send_grads.astype(jnp.bfloat16).reshape(experts_all, capacity, row_width)
    w_first = w_in[0]
    w_second = w_out[0]
    rows_in = lax.all_to_all(send_rows, "exp", split_axis=0, concat_axis=0, tiled=True)
    grads_in = lax.all_to_all(send_grads, "exp", split_axis=0, concat_axis=0, tiled=True)
    lead_count, item_count, width_in = rows_in.shape
    row_total = lead_count * item_count
    row_block = rows_in.reshape(row_total, width_in)
    grad_block = grads_in.reshape(row_total, width_in)
    row_float = row_block.astype(jnp.float32)
    raw_sums = jnp.einsum("rd,dkf->rkf", row_block, w_first, preferred_element_type=jnp.float32)
    back_sums = lax.dot_general(
        grad_block, w_second, (((1,), (1,)), ((), ())), preferred_element_type=jnp.float32
    )
    squares = jnp.sum(row_float * row_float, axis=1)
    square_tile = jnp.broadcast_to(squares[:, None, None], (row_total, 1, head_devices))
    raw_part = lax.psum_scatter(raw_sums, "head", scatter_dimension=2, tiled=True)
    back_part = lax.psum_scatter(back_sums[:, None, :], "head", scatter_dimension=2, tiled=True)
    square_part = lax.psum_scatter(square_tile, "head", scatter_dimension=2, tiled=True)
    norm_scale = lax.rsqrt(square_part[:, 0] / D + norm_eps)
    gate_value = raw_part[:, 0] * norm_scale
    up_value = raw_part[:, 1] * norm_scale
    back_value = back_part[:, 0]
    gate_sigmoid = jax.nn.sigmoid(gate_value)
    gate_silu = gate_value * gate_sigmoid
    act_part = (gate_silu * up_value).astype(jnp.bfloat16)
    grad_gate = back_value * up_value * gate_sigmoid * (1.0 + gate_value * (1.0 - gate_sigmoid))
    grad_up = back_value * gate_silu
    grad_part = jnp.stack([grad_gate, grad_up], axis=1).astype(jnp.bfloat16)
    inner_part = jnp.sum(
        grad_part.astype(jnp.float32) * jnp.stack([gate_value, up_value], axis=1), axis=(1, 2)
    )
    act_whole = lax.all_gather(act_part[:, None, :], "head", axis=2, tiled=True)
    grad_hidden = lax.all_gather(grad_part, "head", axis=2, tiled=True)
    hidden_act = act_whole[:, 0]
    inner_sum = lax.psum(inner_part, "head")
    out_rows = jnp.dot(hidden_act, w_second, preferred_element_type=jnp.float32).astype(
        jnp.bfloat16
    )
    grad_normed = jnp.einsum(
        "rkf,dkf->rd", grad_hidden, w_first, preferred_element_type=jnp.float32
    )
    grad_rows = (
        norm_scale * grad_normed - row_float * (norm_scale * norm_scale / D) * inner_sum[:, None]
    )
    expert_out = out_rows.reshape(lead_count, item_count, width_in)
    expert_grad = grad_rows.astype(jnp.bfloat16).reshape(lead_count, item_count, width_in)
    came_out, came_grad = (
        lax.all_to_all(expert_out, "exp", split_axis=0, concat_axis=0, tiled=True),
        lax.all_to_all(expert_grad, "exp", split_axis=0, concat_axis=0, tiled=True),
    )
    picked_out = came_out.reshape(places, row_width)[place_index].reshape(
        token_count, TOP, row_width
    )
    picked_grad = came_grad.reshape(places, row_width)[place_index].reshape(
        token_count, TOP, row_width
    )
    output = attended.astype(jnp.float32) + jnp.sum(
        route_weights[:, :, None] * picked_out.astype(jnp.float32), axis=1
    )
    grad_attended = grad_out.astype(jnp.float32) + jnp.sum(
        route_weights[:, :, None] * picked_grad.astype(jnp.float32), axis=1
    )
    return (output.astype(jnp.bfloat16), grad_attended.astype(jnp.bfloat16))


def attention_kernel(head_count, group, start_ref, q_ref, k_ref, v_ref, o_ref):
    rows = q_ref.shape[0]
    cached = k_ref.shape[0]
    first = start_ref[0]
    row_pos = first + lax.broadcasted_iota(jnp.int32, (rows, cached), 0)
    visible = lax.broadcasted_iota(jnp.int32, (rows, cached), 1) <= row_pos
    for head in range(head_count):
        cols = slice(head * HEAD_WIDTH, (head + 1) * HEAD_WIDTH)
        kv_head = head // group
        kv_cols = slice(kv_head * HEAD_WIDTH, (kv_head + 1) * HEAD_WIDTH)
        scores = lax.dot_general(
            q_ref[:, cols],
            k_ref[:, kv_cols],
            (((1,), (1,)), ((), ())),
            preferred_element_type=jnp.float32,
        ) * HEAD_WIDTH ** (-0.5)
        scores = jnp.where(visible, scores, hidden_logits)
        best = jnp.max(scores, axis=1, keepdims=True)
        weights = jnp.exp(scores - best)
        total = jnp.sum(weights, axis=1, keepdims=True)
        sums = jnp.dot(
            weights.astype(jnp.bfloat16), v_ref[:, kv_cols], preferred_element_type=jnp.float32
        )
        o_ref[:, cols] = (sums / total).astype(jnp.bfloat16)


def attend_local(queries, key_all, value_all, start):
    head_count = queries.shape[1] // HEAD_WIDTH
    group = head_count // (key_all.shape[1] // HEAD_WIDTH)

    def body(*refs):
        attention_kernel(head_count, group, *refs)

    return pl.pallas_call(
        body,
        out_shape=jax.ShapeDtypeStruct(queries.shape, jnp.bfloat16),
        in_specs=[pl.BlockSpec(memory_space=pltpu.SMEM)]
        + [pl.BlockSpec(memory_space=pltpu.VMEM)] * 3,
        out_specs=pl.BlockSpec(memory_space=pltpu.VMEM),
        name="attention",
    )(start.reshape(1).astype(jnp.int32), queries, key_all, value_all)


def three_parts(value):
    high = value.astype(jnp.bfloat16)
    rest = value - high.astype(jnp.float32)
    middle = rest.astype(jnp.bfloat16)
    low = (rest - middle.astype(jnp.float32)).astype(jnp.bfloat16)
    return high, middle, low


def ring_place(index, count):
    outer, inner = index // 2, index % 2
    return outer + inner * (count - 1 - 2 * outer)


def ring_index(place, count):
    inner = place // (count // 2)
    return 2 * (place + inner * (count - 1 - 2 * place)) + inner


def ring_start(count):
    place = ring_place(lax.axis_index("exp"), count)
    right = ring_index((place + 1) % count, count)
    left = ring_index((place + count - 1) % count, count)
    barrier = pltpu.get_barrier_semaphore()
    for other in (left, right):
        pl.semaphore_signal(
            barrier, inc=1, device_id={"exp": other}, device_id_type=pl.DeviceIdType.MESH
        )
    pl.semaphore_wait(barrier, 2)
    return place, (right, left)


def ring_lanes(count):
    reach = count // 2
    return ((0, 0, reach), (1, 1, reach), (0, 1, reach - 1), (1, 0, reach - 1))


def ring_gather(count, x_ref, out_ref, send_sem, recv_sem, own_sem):
    place, others = ring_start(count)
    me = lax.axis_index("exp")
    rows = x_ref.shape[0]
    half = rows // 2
    own = pltpu.make_async_copy(
        x_ref, out_ref.at[pl.ds(pl.multiple_of(me * rows, rows), rows)], own_sem
    )
    own.start()

    def copy(way, part, step):
        shift = count - step if way == 0 else step
        owner = ring_index((place + shift) % count, count)
        spot = out_ref.at[pl.ds(pl.multiple_of(owner * rows + part * half, half), half)]
        source = x_ref.at[pl.ds(part * half, half)] if step == 0 else spot
        return pltpu.make_async_remote_copy(
            src_ref=source,
            dst_ref=spot,
            send_sem=send_sem.at[way, part, step],
            recv_sem=recv_sem.at[way, part, step],
            device_id={"exp": others[way]},
            device_id_type=pl.DeviceIdType.MESH,
        )

    copies = {}
    for step in range(count // 2):
        for way, part, steps in ring_lanes(count):
            if step < steps:
                if step > 0:
                    copies[way, part, step - 1].wait_recv()
                copies[way, part, step] = copy(way, part, step)
                copies[way, part, step].start()
    for way, part, steps in ring_lanes(count):
        copies[way, part, steps - 1].wait_recv()
    for each in copies.values():
        each.wait_send()
    own.wait()


def ring_scatter(count, x_ref, out_ref, held, send_sem, recv_sem):
    place, others = ring_start(count)
    rows = x_ref.shape[1]
    half = rows // 2

    def term(way, part, step, steps):
        shift = steps - step if way == 0 else count - steps + step
        return x_ref.at[ring_index((place + shift) % count, count), pl.ds(part * half, half)]

    copies = {}
    for step in range(count // 2):
        for way, part, steps in ring_lanes(count):
            if step < steps:
                source = term(way, part, step, steps)
                if step > 0:
                    copies[way, part, step - 1].wait_recv()
                    slot = held.at[way, step - 1, pl.ds(part * half, half)]
                    slot[...] = (
                        slot[...].astype(jnp.float32) + source[...].astype(jnp.float32)
                    ).astype(jnp.bfloat16)
                    source = slot
                copies[way, part, step] = pltpu.make_async_remote_copy(
                    src_ref=source,
                    dst_ref=held.at[way, step, pl.ds(part * half, half)],
                    send_sem=send_sem.at[way, part, step],
                    recv_sem=recv_sem.at[way, part, step],
                    device_id={"exp": others[way]},
                    device_id_type=pl.DeviceIdType.MESH,
                )
                copies[way, part, step].start()
    last = {}
    for way, part, steps in ring_lanes(count):
        copies[way, part, steps - 1].wait_recv()
        last[way, part] = steps - 1
    me = lax.axis_index("exp")
    for part in range(2):
        span = pl.ds(part * half, half)
        out_ref[span] = (
            x_ref[me, span].astype(jnp.float32)
            + held[0, last[0, part], span].astype(jnp.float32)
            + held[1, last[1, part], span].astype(jnp.float32)
        )
    for each in copies.values():
        each.wait_send()


def ring_sems(count):
    return [pltpu.SemaphoreType.DMA((2, 2, count // 2))] * 2


def gather_exp(block, tag):
    count = lax.axis_size("exp")
    rows, width = block.shape

    def gather_body(*refs):
        ring_gather(count, *refs)

    return pl.pallas_call(
        gather_body,
        out_shape=jax.ShapeDtypeStruct((count * rows, width), block.dtype),
        in_specs=[pl.BlockSpec(memory_space=pltpu.VMEM)],
        out_specs=pl.BlockSpec(memory_space=pltpu.VMEM),
        scratch_shapes=ring_sems(count) + [pltpu.SemaphoreType.DMA],
        compiler_params=pltpu.CompilerParams(collective_id=tag, has_side_effects=True),
        name="ring_gather_" + str(tag),
    )(block)


def scatter_exp(blocks, tag):
    count, rows, width = blocks.shape

    def scatter_body(*refs):
        ring_scatter(count, *refs)

    return pl.pallas_call(
        scatter_body,
        out_shape=jax.ShapeDtypeStruct((rows, width), jnp.float32),
        in_specs=[pl.BlockSpec(memory_space=pltpu.VMEM)],
        out_specs=pl.BlockSpec(memory_space=pltpu.VMEM),
        scratch_shapes=[pltpu.VMEM((2, count // 2, rows, width), blocks.dtype)]
        + ring_sems(count),
        compiler_params=pltpu.CompilerParams(collective_id=tag, has_side_effects=True),
        name="ring_scatter",
    )(blocks)


def pair_start():
    me = lax.axis_index("head")
    mate = me + 1 - 2 * (me % 2)
    across = (me + 2) % 4
    barrier = pltpu.get_barrier_semaphore()
    for other in (mate, across):
        pl.semaphore_signal(
            barrier, inc=1, device_id={"head": other}, device_id_type=pl.DeviceIdType.MESH
        )
    pl.semaphore_wait(barrier, 2)
    return me, mate, across


def pair_copy(source, target, send_sem, recv_sem, other):
    copy = pltpu.make_async_remote_copy(
        src_ref=source,
        dst_ref=target,
        send_sem=send_sem,
        recv_sem=recv_sem,
        device_id={"head": other},
        device_id_type=pl.DeviceIdType.MESH,
    )
    copy.start()
    return copy


def pair_scatter(chunks, x_ref, out_ref, near, far, send_sem, recv_sem):
    me, mate, across = pair_start()
    step = x_ref.shape[1] // chunks
    spans = [pl.ds(part * step, step) for part in range(chunks)]
    copies = {}
    for kind, dest in ((0, (mate + 2) % 4), (1, mate)):
        for part, span in enumerate(spans):
            copies[kind, part] = pair_copy(
                x_ref.at[dest, span],
                near.at[kind, span],
                send_sem.at[kind, part],
                recv_sem.at[kind, part],
                mate,
            )
    for part, span in enumerate(spans):
        copies[0, part].wait_recv()
        near[0, span] = (
            near[0, span].astype(jnp.float32) + x_ref[across, span].astype(jnp.float32)
        ).astype(jnp.bfloat16)
        copies[2, part] = pair_copy(
            near.at[0, span], far.at[span], send_sem.at[2, part], recv_sem.at[2, part], across
        )
    for part, span in enumerate(spans):
        copies[1, part].wait_recv()
        copies[2, part].wait_recv()
        out_ref[span] = (
            x_ref[me, span].astype(jnp.float32)
            + near[1, span].astype(jnp.float32)
            + far[span].astype(jnp.float32)
        )
    for each in copies.values():
        each.wait_send()


def pair_gather(chunks, x_ref, out_ref, send_sem, recv_sem, own_sem):
    me, mate, across = pair_start()
    own = pltpu.make_async_copy(x_ref, out_ref.at[me], own_sem)
    own.start()
    step = x_ref.shape[0] // chunks
    spans = [pl.ds(part * step, step) for part in range(chunks)]
    copies = {}
    for kind, other in ((0, across), (1, mate)):
        for part, span in enumerate(spans):
            copies[kind, part] = pair_copy(
                x_ref.at[span],
                out_ref.at[me, span],
                send_sem.at[kind, part],
                recv_sem.at[kind, part],
                other,
            )
    for part, span in enumerate(spans):
        copies[0, part].wait_recv()
        copies[2, part] = pair_copy(
            out_ref.at[across, span],
            out_ref.at[across, span],
            send_sem.at[2, part],
            recv_sem.at[2, part],
            mate,
        )
    for part in range(chunks):
        copies[1, part].wait_recv()
        copies[2, part].wait_recv()
    for each in copies.values():
        each.wait_send()
    own.wait()


def pair_sems(chunks):
    return [pltpu.SemaphoreType.DMA((3, chunks))] * 2


def scatter_head(blocks, tag):
    parts, rows, width = blocks.shape

    def body(*refs):
        pair_scatter(8, *refs)

    return pl.pallas_call(
        body,
        out_shape=jax.ShapeDtypeStruct((rows, width), jnp.float32),
        in_specs=[pl.BlockSpec(memory_space=pltpu.VMEM)],
        out_specs=pl.BlockSpec(memory_space=pltpu.VMEM),
        scratch_shapes=[
            pltpu.VMEM((2, rows, width), blocks.dtype),
            pltpu.VMEM((rows, width), blocks.dtype),
        ]
        + pair_sems(8),
        compiler_params=pltpu.CompilerParams(collective_id=tag, has_side_effects=True),
        name="pair_scatter",
    )(blocks)


def gather_head(block, tag):
    def body(*refs):
        pair_gather(8, *refs)

    return pl.pallas_call(
        body,
        out_shape=jax.ShapeDtypeStruct((4,) + block.shape, block.dtype),
        in_specs=[pl.BlockSpec(memory_space=pltpu.VMEM)],
        out_specs=pl.BlockSpec(memory_space=pltpu.VMEM),
        scratch_shapes=pair_sems(8) + [pltpu.SemaphoreType.DMA],
        compiler_params=pltpu.CompilerParams(collective_id=tag, has_side_effects=True),
        name="pair_gather",
    )(block)


def dense_device(queries, keys, values, w_in, w_out, routes, route_weights, grad_out):
    exp_count = lax.axis_size("exp")
    exp_index = lax.axis_index("exp")
    parts = lax.axis_size("head")
    tokens, width = queries.shape
    experts = w_in.shape[0] * exp_count
    hidden = w_in.shape[3]
    share = hidden // parts
    kv_width = keys.shape[1]
    offset = keys.shape[0] * exp_count - tokens * exp_count
    w_first = w_in[0]
    w_second = w_out[0]
    hits = routes[:, :, None] == jnp.arange(experts, dtype=jnp.int32)[None, None, :]
    table = jnp.sum(jnp.where(hits, route_weights[:, :, None], 0.0), axis=1)
    packed = jnp.concatenate(three_parts(table), axis=1)
    packed = jnp.pad(packed, ((0, 0), (0, -packed.shape[1] % 128)))
    early = gather_exp(jnp.concatenate([keys, values, grad_out, packed], axis=1), 1)
    kv_all = early[:, : 2 * kv_width]
    grad_pack = early[:, 2 * kv_width :]
    grads = grad_pack[:, :width]
    attended = attend_local(
        queries, kv_all[:, :kv_width], kv_all[:, kv_width:], offset + exp_index * tokens
    )
    rows = gather_exp(attended, 2)
    count = rows.shape[0]
    pieces = grad_pack[:, width : width + 3 * experts].astype(jnp.float32)
    table_all = jnp.sum(pieces.reshape(count, 3, experts), axis=1)
    own = (jnp.arange(experts) == exp_index).astype(jnp.float32)
    gain = jnp.sum(table_all * own[None, :], axis=1)[:, None]
    w_split = w_first.reshape(width, 2, parts, share)
    second_split = w_second.reshape(parts, share, width)
    back_sums = jnp.einsum(
        "rd,hfd->hrf", grads, second_split, preferred_element_type=jnp.float32
    ).astype(jnp.bfloat16)
    row_float = rows.astype(jnp.float32)
    raw_sums = jnp.einsum("rd,dkhf->hrkf", rows, w_split, preferred_element_type=jnp.float32)
    raw_sums = raw_sums.astype(jnp.bfloat16).reshape(parts, count, 2 * share)
    squares = jnp.sum(row_float * row_float, axis=1)
    square_tile = jnp.broadcast_to(
        squares.astype(jnp.bfloat16)[None, :, None], (parts, count, -3 * share % 128 + 128 * (share * 3 % 128 == 0))
    )
    raw_part = scatter_head(jnp.concatenate([raw_sums, back_sums, square_tile], axis=2), 4)
    norm_scale = lax.rsqrt(raw_part[:, 3 * share : 3 * share + 1] / D + norm_eps)
    gate_value = raw_part[:, :share] * norm_scale
    up_value = raw_part[:, share : 2 * share] * norm_scale
    back_value = raw_part[:, 2 * share : 3 * share]
    sigmoid = jax.nn.sigmoid(gate_value)
    silu = gate_value * sigmoid
    act = (silu * up_value).astype(jnp.bfloat16)
    grad_gate = (back_value * up_value * sigmoid * (1.0 + gate_value * (1.0 - sigmoid))).astype(
        jnp.bfloat16
    )
    grad_up = (back_value * silu).astype(jnp.bfloat16)
    inner = jnp.sum(
        grad_gate.astype(jnp.float32) * gate_value + grad_up.astype(jnp.float32) * up_value,
        axis=1,
        keepdims=True,
    )
    sent = jnp.concatenate([act, grad_gate, grad_up, *three_parts(inner)], axis=1)
    sent = jnp.pad(sent, ((0, 0), (0, -sent.shape[1] % 128)))
    whole = gather_head(sent, 5)
    inner_sum = jnp.sum(whole[:, :, 3 * share : 3 * share + 3].astype(jnp.float32), axis=(0, 2))[
        :, None
    ]
    out_rows = jnp.einsum(
        "hrf,hfd->rd", whole[:, :, :share], second_split, preferred_element_type=jnp.float32
    )
    grad_pair = whole[:, :, share : 3 * share].reshape(parts, count, 2, share)
    grad_normed = jnp.einsum(
        "hrkf,dkhf->rd", grad_pair, w_split, preferred_element_type=jnp.float32
    )
    grad_rows = norm_scale * grad_normed - row_float * (norm_scale * norm_scale / D) * inner_sum
    routed = gain > 0.0
    both = jnp.concatenate(
        [
            jnp.where(routed, gain * out_rows, 0.0).astype(jnp.bfloat16),
            jnp.where(routed, gain * grad_rows, 0.0).astype(jnp.bfloat16),
        ],
        axis=1,
    )
    summed = scatter_exp(both.reshape(exp_count, tokens, 2 * width), 3)
    output = attended.astype(jnp.float32) + summed[:, :width]
    grad_attended = grad_out.astype(jnp.float32) + summed[:, width:]
    return (output.astype(jnp.bfloat16), grad_attended.astype(jnp.bfloat16))


def solution(mesh):
    dense = 2 * TOP >= mesh.shape["exp"] and mesh.shape["exp"] % 2 == 0 and mesh.shape["head"] == 4
    in_specs = (
        P("exp", "head"),
        P("exp", "head"),
        P("exp", "head"),
        P("exp", "head", None, None),
        P("exp", None, "head"),
        P("exp", None),
        P("exp", None),
        P("exp", "head"),
    )
    out_specs = (P("exp", "head"), P("exp", "head"))
    return jax.shard_map(
        dense_device if dense else per_device, mesh=mesh, in_specs=in_specs, out_specs=out_specs, check_vma=False
    )
```
